32 devices in a mesh: ctx: 8 (over z, x), dp: 4 (over y, core).
Axes of the slice: x: 2, y: 2, z: 4, core: 2. Of those that a mesh axis runs over, the one named last changes fastest.
Arguments:
- queries: bfloat16 [4, 2048, 1024], P('dp', 'ctx'), may hold values from -8 to 8
- keys: bfloat16 [4, 2048, 1024], P('dp', 'ctx'), may hold values from -8 to 8
- values: bfloat16 [4, 2048, 1024], P('dp', 'ctx'), may hold values from -6 to 6
- cotangent: bfloat16 [4, 2048, 2048], P('dp', 'ctx'), may hold values from -6 to 6
- proj_weight: bfloat16 [1024, 2048], P('dp'), may hold values from -0.1875 to 0.1875
- pattern: int32 [4, 8, 16, 2], P('dp'), may hold values 0 or 1
Outputs:
- projected: bfloat16 [4, 2048, 2048], P('dp', 'ctx')
- grad_query: bfloat16 [4, 2048, 1024], P('dp', 'ctx')
- grad_key: bfloat16 [4, 2048, 1024], P('dp', 'ctx')
- grad_value: bfloat16 [4, 2048, 1024], P('dp', 'ctx')
- grad_proj: float32 [1024, 2048], P('dp', 'ctx')
The draws below stay inside these ranges and needn't reach their ends.
Inputs may be any that keep to these rules, and one draw needn't show every extreme that they name: `pattern`: entries with o = 0 or with q - o < 1 are not read.
All inputs are finite; a program needn't handle non-finite values. No bound on the sum of `pattern` on one device may be relied on, other than what follows from the above.
Results may differ from the reference program's by a relative error of at most 0.0085.
The reference program's roundings to bfloat16 on the way count: a program that leaves them out, or rounds other values in their place, can miss the bound.
Values may be sent and summed in bfloat16 or wider, within the bound.
No kernel may reach another device: no remote copies, remote signals or barrier semaphores. Data moves between devices by JAX's collectives and lax.ppermute only.
A program may use at most 128 MiB of HBM per device.

```python
import jax
import jax.numpy as jnp
from jax import lax

WIDTH = 2048
HEADS = 8
HDIM = 128
BLK = 128
TOK_DEV = 256
HW = 1024
BLK_DEV = 2
WIN = 2
SEQ = 2048
NQB = 16
DOCS = 4
N_CTX = 8


def query_key_pair(key):
    shape = (DOCS, SEQ, HEADS * HDIM)
    base_query = jax.random.normal(jax.random.fold_in(key, 101), shape, jnp.float32)
    base_key = jax.random.normal(jax.random.fold_in(key, 202), shape, jnp.float32)
    return (jnp.clip(base_query, -8.0, 8.0), jnp.clip(base_key, -8.0, 8.0))


def draw_queries(key, part):
    return query_key_pair(key)[0].astype(jnp.bfloat16)


def draw_keys(key, part):
    return query_key_pair(key)[1].astype(jnp.bfloat16)


def plant(result, own_key, least, top_value):
    longest = result.shape.index(max(result.shape))
    spots = []
    for shift in (0, 1):
        where = [jax.random.randint(jax.random.fold_in(own_key, axis), (), 0, length) for axis, length in enumerate(result.shape)]
        where[longest] = (where[longest] + shift) % result.shape[longest]
        spots.append(tuple(where))
    return result.at[spots[0]].set(least).at[spots[1]].set(top_value)


def spiked(array, own_key, source, target, shards_of, factor):
    def block_of(dim):
        return (jnp.arange(array.shape[dim]) // (array.shape[dim] // shards_of)).reshape((-1,) + (1,) * (array.ndim - 1 - dim))

    near = jax.random.permutation(own_key, shards_of)[block_of(target)]
    second = (block_of(target) + shards_of // 2) % shards_of
    return jnp.where((block_of(source) == near) | (block_of(source) == second), factor * array, array)


def level_of(rng, extent, split, smallest, high):
    def one(axis_at, shards_of):
        steps = jax.random.uniform(jax.random.fold_in(jax.random.fold_in(rng, 6), axis_at), (shards_of,), jnp.float32, smallest / len(split), high / len(split))
        return jnp.repeat(jnp.exp(steps), extent[axis_at] // shards_of).reshape((-1,) + (1,) * (len(extent) - axis_at - 1))

    loudness = one(*split[0])
    for cut in split[1:]:
        loudness = loudness * one(*cut)
    return loudness


def normal_values(rng, shape, deviation, bound, cuts=(), kind=jnp.bfloat16):
    drawn = deviation * jax.random.normal(rng, shape, jnp.float32)
    if cuts:
        drawn = drawn * level_of(rng, shape, cuts, -0.22, 0.18)
    return jnp.clip(drawn, -bound, bound).astype(kind)


def bell_draw_with(stream_key, shape, spread, bound, shards, heavy, held_as=jnp.bfloat16):
    drawn = spread * jax.random.normal(stream_key, shape, jnp.float32)
    if shards:
        drawn = drawn * level_of(stream_key, shape, shards, -0.22, 0.18)
    return jnp.clip(spiked(drawn, jax.random.fold_in(stream_key, 3), *heavy), -bound, bound).astype(held_as)


def setup_inputs(seed: int = 0) -> dict:
    splits = jax.random.split(jax.random.key(seed), 7)
    return {
        "queries": draw_queries(jax.random.fold_in(splits[6], 71), 0),
        "keys": draw_keys(jax.random.fold_in(splits[6], 71), 0),
        "values": normal_values(splits[2], (DOCS, SEQ, HW), 1.0, 6.0, ((0, 4), (1, 8))),
        "cotangent": bell_draw_with(splits[3], (DOCS, SEQ, WIDTH), 1.0, 6.0, ((0, 4), (1, 8)), (1, 2, 8, 2.0)),
        "proj_weight": normal_values(splits[4], (HW, WIDTH), HW ** -0.5, 0.1875, ((0, 4),)),
        "pattern": plant((jax.random.randint(splits[5], (DOCS, HEADS, NQB, WIN), 0, 2) < 1).astype(jnp.int32), jax.random.fold_in(splits[5], 1), 0, 1),
    }


masked_value = -1.0e30


def product(form, left, right):
    return jnp.einsum(form, left.astype(jnp.float32), right.astype(jnp.float32))


def block_masks(pattern_rows, query_blocks):
    column = jnp.arange(WIN * BLK, dtype=jnp.int32)
    within = jnp.arange(BLK, dtype=jnp.int32)
    offsets = WIN - 1 - jnp.arange(WIN, dtype=jnp.int32)
    flipped = jnp.flip(pattern_rows, axis=2) == 1
    key_blocks = query_blocks[:, None] - offsets[None, :]
    permitted = (flipped | (offsets == 0)[None, None, :]) & (key_blocks >= 1)[:, None, :]
    expanded = jnp.repeat(permitted, BLK, axis=2)
    causal = (column[None, :] < (WIN - 1) * BLK) | (column[None, :] - (WIN - 1) * BLK <= within[:, None])
    key_mask = expanded[:, :, None, :] & causal[None, None, :, :]
    sink_mask = (query_blocks[:, None, None] > 0) | (within[None, None, :] <= within[None, :, None])
    return key_mask, sink_mask[:, None, :, :]


def attend_scores(queries_b, key_window, sink_keys, key_mask, sink_mask, product):
    inverse_root = HDIM ** -0.5
    scores = product('nqhd,nkhd->nhqk', queries_b, key_window) * inverse_root
    sink_scores = product('nqhd,khd->nhqk', queries_b, sink_keys) * inverse_root
    return jnp.where(key_mask, scores, masked_value), jnp.where(sink_mask, sink_scores, masked_value)


def forward_blocks(queries_b, key_window, value_window, sink_keys, sink_values, key_mask, sink_mask, product):
    scores, sink_scores = attend_scores(queries_b, key_window, sink_keys, key_mask, sink_mask, product)
    row_max = jnp.maximum(jnp.max(scores, axis=-1), jnp.max(sink_scores, axis=-1))
    row_total = jnp.sum(jnp.exp(scores - row_max[..., None]), axis=-1) + jnp.sum(jnp.exp(sink_scores - row_max[..., None]), axis=-1)
    log_total = row_max + jnp.log(row_total)
    weights = jnp.exp(scores - log_total[..., None]).astype(jnp.bfloat16)
    sink_weights = jnp.exp(sink_scores - log_total[..., None]).astype(jnp.bfloat16)
    attended = product('nhqk,nkhd->nqhd', weights, value_window) + product('nhqk,khd->nqhd', sink_weights, sink_values)
    return attended.astype(jnp.bfloat16), log_total


def backward_blocks(queries_b, key_window, value_window, sink_keys, sink_values, key_mask, sink_mask, log_total, out_grad, row_delta, product):
    inverse_root = HDIM ** -0.5
    scores, sink_scores = attend_scores(queries_b, key_window, sink_keys, key_mask, sink_mask, product)
    weights = jnp.exp(scores - log_total[..., None])
    sink_weights = jnp.exp(sink_scores - log_total[..., None])
    prob_grad = product('nqhd,nkhd->nhqk', out_grad, value_window)
    sink_prob_grad = product('nqhd,khd->nhqk', out_grad, sink_values)
    score_grad = (weights * (prob_grad - row_delta[..., None])).astype(jnp.bfloat16)
    sink_score_grad = (sink_weights * (sink_prob_grad - row_delta[..., None])).astype(jnp.bfloat16)
    query_grad = inverse_root * (product('nhqk,nkhd->nqhd', score_grad, key_window) + product('nhqk,khd->nqhd', sink_score_grad, sink_keys))
    window_key_grad = inverse_root * product('nhqk,nqhd->nkhd', score_grad, queries_b)
    window_value_grad = product('nhqk,nqhd->nkhd', weights.astype(jnp.bfloat16), out_grad)
    sink_key_grad = inverse_root * product('nhqk,nqhd->khd', sink_score_grad, queries_b)
    sink_value_grad = product('nhqk,nqhd->khd', sink_weights.astype(jnp.bfloat16), out_grad)
    return query_grad, window_key_grad, window_value_grad, sink_key_grad, sink_value_grad


def make_windows(extended, first):
    pieces = [extended[(number + first) * BLK:(number + first + WIN) * BLK] for number in range(BLK_DEV)]
    return jnp.stack(pieces).reshape(BLK_DEV, WIN * BLK, HEADS, HDIM)


def place_windows(window_grad):
    flat = window_grad.reshape(BLK_DEV, WIN * BLK, HEADS * HDIM)
    placed = jnp.zeros((2 * BLK_DEV * BLK, HEADS * HDIM), jnp.float32)
    for number in range(BLK_DEV):
        placed = placed + jnp.pad(flat[number], (((number + 1) * BLK, (2 * BLK_DEV - number - 1 - WIN) * BLK), (0, 0)))
    return placed


def one_document(queries, keys, values, cotangent, pattern, proj_weight):
    width_heads = HEADS * HDIM
    zero_rows = jnp.zeros((TOK_DEV, width_heads), keys.dtype)
    key_pad = jnp.concatenate([zero_rows, keys], axis=0)
    value_pad = jnp.concatenate([zero_rows, values], axis=0)
    sink_keys = keys[:BLK].reshape(BLK, HEADS, HDIM)
    sink_values = values[:BLK].reshape(BLK, HEADS, HDIM)

    def group_inputs(group):
        start = (group * TOK_DEV).astype(jnp.int32)
        key_window = make_windows(lax.dynamic_slice_in_dim(key_pad, start, 2 * TOK_DEV, 0), 1)
        value_window = make_windows(lax.dynamic_slice_in_dim(value_pad, start, 2 * TOK_DEV, 0), 1)
        query_rows = lax.dynamic_slice_in_dim(queries, start, TOK_DEV, 0).reshape(BLK_DEV, BLK, HEADS, HDIM)
        query_blocks = (group * BLK_DEV + jnp.arange(BLK_DEV, dtype=jnp.int32)).astype(jnp.int32)
        pattern_rows = jnp.transpose(lax.dynamic_slice_in_dim(pattern, (group * BLK_DEV).astype(jnp.int32), BLK_DEV, 1), (1, 0, 2))
        key_mask, sink_mask = block_masks(pattern_rows, query_blocks)
        return query_rows, key_window, value_window, key_mask, sink_mask

    def forward_group(group):
        query_rows, key_window, value_window, key_mask, sink_mask = group_inputs(group)
        return forward_blocks(query_rows, key_window, value_window, sink_keys, sink_values, key_mask, sink_mask, product)

    groups = jnp.arange(N_CTX, dtype=jnp.int32)
    attended, log_total = lax.map(forward_group, groups)
    attended_rows = attended.reshape(SEQ, width_heads)
    projected = jnp.dot(attended_rows, proj_weight, preferred_element_type=jnp.float32).astype(jnp.bfloat16)
    grad_attended = jnp.dot(cotangent, proj_weight.T, preferred_element_type=jnp.float32).astype(jnp.bfloat16)
    weight_term = jnp.dot(attended_rows.T, cotangent, preferred_element_type=jnp.float32)
    row_delta = jnp.sum(grad_attended.astype(jnp.float32).reshape(SEQ, HEADS, HDIM) * attended_rows.astype(jnp.float32).reshape(SEQ, HEADS, HDIM), axis=-1)
    delta_groups = jnp.transpose(row_delta.reshape(N_CTX, BLK_DEV, BLK, HEADS), (0, 1, 3, 2))
    grad_groups = grad_attended.reshape(N_CTX, BLK_DEV, BLK, HEADS, HDIM)

    def backward_step(carry, inputs):
        key_acc, value_acc, sink_key_acc, sink_value_acc = carry
        group, group_lse, group_grad, group_delta = inputs
        query_rows, key_window, value_window, key_mask, sink_mask = group_inputs(group)
        query_grad, window_key, window_value, sink_key, sink_value = backward_blocks(
            query_rows, key_window, value_window, sink_keys, sink_values, key_mask, sink_mask,
            group_lse, group_grad, group_delta, product)
        start = (group * TOK_DEV).astype(jnp.int32)
        key_acc = lax.dynamic_update_slice_in_dim(key_acc, lax.dynamic_slice_in_dim(key_acc, start, 2 * TOK_DEV, 0) + place_windows(window_key), start, 0)
        value_acc = lax.dynamic_update_slice_in_dim(value_acc, lax.dynamic_slice_in_dim(value_acc, start, 2 * TOK_DEV, 0) + place_windows(window_value), start, 0)
        return (key_acc, value_acc, sink_key_acc + sink_key, sink_value_acc + sink_value), query_grad

    initial = (jnp.zeros((SEQ + TOK_DEV, width_heads), jnp.float32), jnp.zeros((SEQ + TOK_DEV, width_heads), jnp.float32),
               jnp.zeros((BLK, HEADS, HDIM), jnp.float32), jnp.zeros((BLK, HEADS, HDIM), jnp.float32))
    carry, query_grads = lax.scan(backward_step, initial, (groups, log_total, grad_groups, delta_groups))
    key_grad = carry[0][TOK_DEV:]
    value_grad = carry[1][TOK_DEV:]
    key_grad = jnp.concatenate([key_grad[:BLK] + carry[2].reshape(BLK, width_heads), key_grad[BLK:]], axis=0)
    value_grad = jnp.concatenate([value_grad[:BLK] + carry[3].reshape(BLK, width_heads), value_grad[BLK:]], axis=0)
    return (projected, query_grads.reshape(SEQ, width_heads).astype(jnp.bfloat16),
            key_grad.astype(jnp.bfloat16), value_grad.astype(jnp.bfloat16), weight_term)


def reference(queries, keys, values, cotangent, proj_weight, pattern):
    def per_document(items):
        return one_document(items[0], items[1], items[2], items[3], items[4], proj_weight)

    projected, grad_query, grad_key, grad_value, terms = lax.map(per_document, (queries, keys, values, cotangent, pattern))
    grad_proj = jnp.sum(terms, axis=0) * (DOCS * SEQ) ** -0.5
    return (projected, grad_query, grad_key, grad_value, grad_proj)
```

```python
import functools

import jax
import jax.numpy as jnp
from jax import lax
from jax.experimental import pallas as pl
from jax.experimental.pallas import tpu as pltpu
from jax.sharding import PartitionSpec as P

HDIM = 128
BLK = 128
WIN = 2
HEADS_STEP = 2

MASKED = -1e30
ROOT = HDIM ** (-0.5)
F32 = jnp.float32
BF16 = jnp.bfloat16


def dot(left, right, left_dim, right_dim):
    return lax.dot_general(
        left, right, (((left_dim,), (right_dim,)), ((), ())), preferred_element_type=F32
    )


def probabilities(q, k_ext, k_sink, pattern_ref, head, first_block):
    blocks = q.shape[0] // BLK
    row = lax.broadcasted_iota(jnp.int32, (BLK, BLK), 0)
    column = lax.broadcasted_iota(jnp.int32, (BLK, BLK), 1)
    causal = column <= row
    sink_scores = dot(q, k_sink, 1, 1) * ROOT
    window, sink = [], []
    for number in range(blocks):
        here = slice(number * BLK, (number + 1) * BLK)
        block = first_block + number
        scores = dot(q[here], k_ext[number * BLK : (number + WIN) * BLK], 1, 1) * ROOT
        reached = jnp.logical_and(pattern_ref[0, head, block, 1] == 1, block >= 2)
        before = jnp.where(reached, scores[:, :BLK], MASKED)
        own = jnp.where(jnp.logical_and(causal, block >= 1), scores[:, BLK:], MASKED)
        first = jnp.where(jnp.logical_or(causal, block >= 1), sink_scores[here], MASKED)
        top = jnp.max(jnp.maximum(jnp.maximum(before, own), first), axis=1, keepdims=True)
        before = jnp.exp(before - top)
        own = jnp.exp(own - top)
        first = jnp.exp(first - top)
        total = jnp.sum(before + own + first, axis=1, keepdims=True)
        inverse = 1.0 / total
        window.append(jnp.concatenate([before * inverse, own * inverse], axis=1))
        sink.append(first * inverse)
    return window, jnp.concatenate(sink, axis=0)


def forward_kernel(q_ref, k_ref, v_ref, before_ref, sink_k_ref, sink_v_ref, pattern_ref, out_ref):
    rows = q_ref.shape[0]
    blocks = rows // BLK
    first_block = lax.axis_index("ctx") * blocks
    for local in range(q_ref.shape[1] // HDIM):
        cols = slice(local * HDIM, (local + 1) * HDIM)
        head = pl.program_id(0) * (q_ref.shape[1] // HDIM) + local
        k_ext = jnp.concatenate([before_ref[:BLK, cols], k_ref[:, cols]], axis=0)
        v_ext = jnp.concatenate([before_ref[BLK:, cols], v_ref[:, cols]], axis=0)
        window, sink = probabilities(
            q_ref[:, cols], k_ext, sink_k_ref[:, cols], pattern_ref, head, first_block
        )
        from_sink = dot(sink.astype(BF16), sink_v_ref[:, cols], 1, 0)
        for number in range(blocks):
            here = slice(number * BLK, (number + 1) * BLK)
            near = dot(
                window[number].astype(BF16), v_ext[number * BLK : (number + WIN) * BLK], 1, 0
            )
            out_ref[here, cols] = (near + from_sink[here]).astype(BF16)


def backward_kernel(
    q_ref,
    k_ref,
    v_ref,
    before_ref,
    sink_k_ref,
    sink_v_ref,
    pattern_ref,
    attn_ref,
    grad_ref,
    dq_ref,
    dk_ref,
    dv_ref,
    dbefore_ref,
    dsink_k_ref,
    dsink_v_ref,
):
    rows = q_ref.shape[0]
    blocks = rows // BLK
    first_block = lax.axis_index("ctx") * blocks
    for local in range(q_ref.shape[1] // HDIM):
        cols = slice(local * HDIM, (local + 1) * HDIM)
        head = pl.program_id(0) * (q_ref.shape[1] // HDIM) + local
        q = q_ref[:, cols]
        grad = grad_ref[:, cols]
        k_sink = sink_k_ref[:, cols]
        k_ext = jnp.concatenate([before_ref[:BLK, cols], k_ref[:, cols]], axis=0)
        v_ext = jnp.concatenate([before_ref[BLK:, cols], v_ref[:, cols]], axis=0)
        window, sink = probabilities(q, k_ext, k_sink, pattern_ref, head, first_block)
        delta = jnp.sum(grad.astype(F32) * attn_ref[:, cols].astype(F32), axis=1, keepdims=True)
        dprobs = dot(grad, sink_v_ref[:, cols], 1, 1)
        dscores = (sink * (dprobs - delta)).astype(BF16)
        dq_sink = dot(dscores, k_sink, 1, 0)
        dsink_k_ref[:, cols] = (dot(dscores, q, 0, 0) * ROOT).astype(dsink_k_ref.dtype)
        dsink_v_ref[:, cols] = dot(sink.astype(BF16), grad, 0, 0).astype(dsink_v_ref.dtype)
        dk_parts = [None] * (blocks + 1)
        dv_parts = [None] * (blocks + 1)
        for number in range(blocks):
            here = slice(number * BLK, (number + 1) * BLK)
            there = slice(number * BLK, (number + WIN) * BLK)
            dprobs = dot(grad[here], v_ext[there], 1, 1)
            dscores = (window[number] * (dprobs - delta[here])).astype(BF16)
            dq = dot(dscores, k_ext[there], 1, 0)
            dq_ref[here, cols] = ((dq + dq_sink[here]) * ROOT).astype(BF16)
            dk = dot(dscores, q[here], 0, 0) * ROOT
            dv = dot(window[number].astype(BF16), grad[here], 0, 0)
            for part in range(WIN):
                piece = slice(part * BLK, (part + 1) * BLK)
                at = number + part
                dk_parts[at] = dk[piece] if dk_parts[at] is None else dk_parts[at] + dk[piece]
                dv_parts[at] = dv[piece] if dv_parts[at] is None else dv_parts[at] + dv[piece]
        dbefore_ref[:BLK, cols] = dk_parts[0].astype(dbefore_ref.dtype)
        dbefore_ref[BLK:, cols] = dv_parts[0].astype(dbefore_ref.dtype)
        dk_ref[:, cols] = jnp.concatenate(dk_parts[1:], axis=0)
        dv_ref[:, cols] = jnp.concatenate(dv_parts[1:], axis=0)


def head_spec(rows):
    return pl.BlockSpec((rows, HEADS_STEP * HDIM), lambda step: (0, step))


def whole_smem(shape):
    return pl.BlockSpec(shape, lambda *_: (0,) * len(shape), memory_space=pltpu.SMEM)


def attention_specs(rows, pattern):
    return [
        head_spec(rows),
        head_spec(rows),
        head_spec(rows),
        head_spec(2 * BLK),
        head_spec(BLK),
        head_spec(BLK),
        whole_smem(pattern.shape),
    ]


def attention_forward(q, k, v, before, sink_k, sink_v, pattern):
    rows, width = q.shape
    return pl.pallas_call(
        forward_kernel,
        grid=(width // (HEADS_STEP * HDIM),),
        in_specs=attention_specs(rows, pattern),
        out_specs=head_spec(rows),
        out_shape=jax.ShapeDtypeStruct((rows, width), BF16),
        name="attention_forward",
    )(q, k, v, before, sink_k, sink_v, pattern)


def attention_backward(q, k, v, before, sink_k, sink_v, pattern, attn, grad):
    rows, width = q.shape
    shape = jax.ShapeDtypeStruct
    return pl.pallas_call(
        backward_kernel,
        grid=(width // (HEADS_STEP * HDIM),),
        in_specs=attention_specs(rows, pattern) + [head_spec(rows), head_spec(rows)],
        out_specs=[
            head_spec(rows),
            head_spec(rows),
            head_spec(rows),
            head_spec(2 * BLK),
            head_spec(BLK),
            head_spec(BLK),
        ],
        out_shape=[
            shape((rows, width), BF16),
            shape((rows, width), F32),
            shape((rows, width), F32),
            shape((2 * BLK, width), BF16),
            shape((BLK, width), F32),
            shape((BLK, width), F32),
        ],
        name="attention_backward",
    )(q, k, v, before, sink_k, sink_v, pattern, attn, grad)


def grad_attn_kernel(count, *refs):
    cot_ref, pieces, out_ref = refs[0], refs[1:-1], refs[-1]
    mine = lax.axis_index("dp")
    number = 0
    for piece in pieces:
        depth = piece.shape[1]
        for slot in range(piece.shape[0]):
            at = pl.multiple_of((mine ^ order_of(count)[number]) * depth, HDIM)
            out_ref[:, pl.ds(at, depth)] = dot(cot_ref[...], piece[slot], 1, 1).astype(BF16)
            number += 1


def projected_kernel(count, *refs):
    attn_ref, pieces, out_ref = refs[0], refs[1:-1], refs[-1]
    mine = lax.axis_index("dp")
    total, number = None, 0
    for piece in pieces:
        depth = piece.shape[1]
        for slot in range(piece.shape[0]):
            at = pl.multiple_of((mine ^ order_of(count)[number]) * depth, HDIM)
            term = dot(attn_ref[:, pl.ds(at, depth)], piece[slot], 1, 0)
            total = term if total is None else total + term
            number += 1
    out_ref[...] = total.astype(BF16)


def weight_grad_kernel(scale, pairs, *refs):
    lefts, rights, out_ref = refs[:pairs], refs[pairs : 2 * pairs], refs[-1]
    total = None
    for left, right in zip(lefts, rights):
        for slot in range(left.shape[0]):
            term = dot(left[slot], right[slot], 0, 0)
            total = term if total is None else total + term
    out_ref[0] = total * scale


def grad_attn_of(cot, pieces, count):
    rows = cot.shape[0]
    width = count * pieces[0].shape[1]
    return pl.pallas_call(
        functools.partial(grad_attn_kernel, count),
        out_shape=jax.ShapeDtypeStruct((rows, width), BF16),
        name="grad_attn",
    )(cot, *pieces)


def projected_of(attn, pieces, count):
    return pl.pallas_call(
        functools.partial(projected_kernel, count),
        out_shape=jax.ShapeDtypeStruct((attn.shape[0], pieces[0].shape[2]), BF16),
        name="projected",
    )(attn, *pieces)


def weight_grad_of(attn_pieces, cot_pieces, scale, count):
    features = attn_pieces[0].shape[2]
    wanted = cot_pieces[0].shape[2] // count
    columns = max(wanted, HDIM)
    chunks = cot_pieces[0].shape[2] // columns
    terms = pl.pallas_call(
        functools.partial(weight_grad_kernel, scale, len(attn_pieces)),
        grid=(chunks,),
        in_specs=[pl.BlockSpec(a.shape, lambda step: (0, 0, 0)) for a in attn_pieces]
        + [pl.BlockSpec(c.shape[:2] + (columns,), lambda step: (0, 0, step)) for c in cot_pieces],
        out_specs=pl.BlockSpec((1, features, columns), lambda step: (step, 0, 0)),
        out_shape=jax.ShapeDtypeStruct((chunks, features, columns), F32),
        name="weight_grad",
    )(*attn_pieces, *cot_pieces)
    if columns == wanted:
        return terms
    terms = terms.reshape(chunks, features, columns // wanted, wanted)
    return jnp.swapaxes(terms, 1, 2).reshape(count, features, wanted)


def bits_of(count):
    return [1 << place for place in range(count.bit_length() - 1)]


def order_of(count):
    order = [0]
    for bit in reversed(bits_of(count)):
        order += [one ^ bit for one in order]
    return order


def swap(value, axis, count, bit):
    return lax.ppermute(value, axis, [(one, one ^ bit) for one in range(count)])


def gather_pieces(value, axis, count):
    pieces = [value[None]]
    for bit in reversed(bits_of(count)):
        held = pieces[0] if len(pieces) == 1 else jnp.concatenate(pieces, axis=0)
        pieces.append(swap(held, axis, count, bit))
    return pieces


def exchange_columns(value, axis, count):
    mine = lax.axis_index(axis)
    columns = value.shape[1] // count
    pieces = [value[None]]
    for bit in reversed(bits_of(count)):
        half = bit * columns
        upper = (mine & bit) != 0
        keep = jnp.where(upper, half, 0)
        away = half - keep
        held = pieces[0] if len(pieces) == 1 else jnp.concatenate(pieces, axis=0)
        got = swap(lax.dynamic_slice_in_dim(held, away, half, 2), axis, count, bit)
        pieces = [lax.dynamic_slice_in_dim(one, keep, half, 2) for one in pieces] + [got]
    return pieces


def spread_first(value, axis, count, order):
    mine = lax.axis_index(axis)
    covered = 0
    for bit in order:
        pairs = [(one, one | bit) for one in range(count) if one & ~covered == 0]
        got = lax.ppermute(value, axis, pairs)
        value = jnp.where((mine & bit) != 0, got, value)
        covered |= bit
    return value


def sum_to_first(value, axis, count, order):
    done = 0
    for bit in order:
        pairs = [(one, one ^ bit) for one in range(count) if one & bit and one & done == 0]
        value = value + lax.ppermute(value.astype(BF16), axis, pairs).astype(F32)
        done |= bit
    return value


def sum_scatter(value, axis, count):
    mine = lax.axis_index(axis)
    bits = bits_of(count)
    value = value.reshape((2,) * len(bits) + value.shape[1:])
    for place, bit in enumerate(bits):
        dim = len(bits) - 1 - place
        here = jnp.where((mine & bit) != 0, 1, 0)
        away = lax.dynamic_index_in_dim(value, 1 - here, dim, keepdims=False)
        got = swap(away.astype(BF16), axis, count, bit)
        value = lax.dynamic_index_in_dim(value, here, dim, keepdims=False) + got.astype(F32)
    return value


def body(context_count, document_count, queries, keys, values, cotangent, proj_weight, pattern):
    q, k, v, cot = queries[0], keys[0], values[0], cotangent[0]
    rows, width = q.shape
    context = lax.axis_index("ctx")
    ctx_bits = bits_of(context_count)
    far_first = ctx_bits[:0:-1]

    last = jnp.concatenate([k[rows - BLK :], v[rows - BLK :]], axis=0)
    before = lax.ppermute(last, "ctx", [(one, one + 1) for one in range(context_count - 1)])
    sink_k = spread_first(k[:BLK], "ctx", context_count, ctx_bits[:1] + far_first)
    sink_v = spread_first(v[:BLK], "ctx", context_count, far_first + ctx_bits[:1])
    weights = gather_pieces(proj_weight, "dp", document_count)
    cots = gather_pieces(cot, "dp", document_count)

    grad_attn = grad_attn_of(cot, weights, document_count)
    attn = attention_forward(q, k, v, before, sink_k, sink_v, pattern)
    attns = exchange_columns(attn, "dp", document_count)
    dq, dk, dv, dbefore, dsink_k, dsink_v = attention_backward(
        q, k, v, before, sink_k, sink_v, pattern, attn, grad_attn
    )
    later = lax.ppermute(dbefore, "ctx", [(one + 1, one) for one in range(context_count - 1)])
    sink_k_sum = sum_to_first(dsink_k, "ctx", context_count, ctx_bits)
    sink_v_sum = sum_to_first(dsink_v, "ctx", context_count, ctx_bits[1:] + ctx_bits[:1])
    projected = projected_of(attn, weights, document_count)
    scale = float(rows * context_count * document_count) ** (-0.5)
    terms = weight_grad_of(attns, cots, scale, context_count)
    grad_proj = sum_scatter(terms, "ctx", context_count)

    def joined(own, back, first):
        first = jnp.where(context == 0, first, 0.0)
        head = own[:BLK] + first
        tail = own[rows - BLK :] + back.astype(F32)
        return jnp.concatenate([head, own[BLK : rows - BLK], tail], axis=0).astype(BF16)

    return (
        projected[None],
        dq[None],
        joined(dk, later[:BLK], sink_k_sum)[None],
        joined(dv, later[BLK:], sink_v_sum)[None],
        grad_proj,
    )


def solution(mesh):
    return jax.shard_map(
        functools.partial(body, mesh.shape["ctx"], mesh.shape["dp"]),
        mesh=mesh,
        in_specs=(
            P("dp", "ctx", None),
            P("dp", "ctx", None),
            P("dp", "ctx", None),
            P("dp", "ctx", None),
            P("dp", None),
            P("dp", None, None, None),
        ),
        out_specs=(
            P("dp", "ctx", None),
            P("dp", "ctx", None),
            P("dp", "ctx", None),
            P("dp", "ctx", None),
            P("dp", "ctx"),
        ),
        check_vma=False,
    )
```

```python
import functools

import jax
import jax.numpy as jnp
from jax import lax
from jax.experimental import pallas as pl
from jax.experimental.pallas import tpu as pltpu
from jax.sharding import PartitionSpec as P


HDIM = 128
BLK = 128

WIN = 2
HEADS_STEP = 2

MASKED = -1e30
ROOT = HDIM ** (-0.5)
F32 = jnp.float32
BF16 = jnp.bfloat16


def dot(left, right, left_dim, right_dim):
    return lax.dot_general(
        left, right, (((left_dim,), (right_dim,)), ((), ())), preferred_element_type=F32
    )


def probabilities(q, k_ext, k_sink, pattern_ref, head, first_block):
    blocks = q.shape[0] // BLK
    row = lax.broadcasted_iota(jnp.int32, (BLK, BLK), 0)
    column = lax.broadcasted_iota(jnp.int32, (BLK, BLK), 1)
    causal = column <= row
    sink_scores = dot(q, k_sink, 1, 1) * ROOT
    window, sink = [], []
    for number in range(blocks):
        here = slice(number * BLK, (number + 1) * BLK)
        block = first_block + number
        scores = dot(q[here], k_ext[number * BLK : (number + WIN) * BLK], 1, 1) * ROOT
        reached = jnp.logical_and(pattern_ref[0, head, block, 1] == 1, block >= 2)
        before = jnp.where(reached, scores[:, :BLK], MASKED)
        own = jnp.where(jnp.logical_and(causal, block >= 1), scores[:, BLK:], MASKED)
        first = jnp.where(jnp.logical_or(causal, block >= 1), sink_scores[here], MASKED)
        top = jnp.max(jnp.maximum(jnp.maximum(before, own), first), axis=1, keepdims=True)
        before = jnp.exp(before - top)
        own = jnp.exp(own - top)
        first = jnp.exp(first - top)
        total = jnp.sum(before + own + first, axis=1, keepdims=True)
        inverse = 1.0 / total
        window.append(jnp.concatenate([before * inverse, own * inverse], axis=1))
        sink.append(first * inverse)
    return window, jnp.concatenate(sink, axis=0)


def forward_kernel(
    count,
    q_ref,
    k_ref,
    v_ref,
    before_ref,
    sink_k_ref,
    sink_v_ref,
    pattern_ref,
    out_ref,
    *away_refs,
):
    rows = q_ref.shape[0]
    blocks = rows // BLK
    first_block = lax.axis_index("ctx") * blocks
    for local in range(q_ref.shape[1] // HDIM):
        cols = slice(local * HDIM, (local + 1) * HDIM)
        head = pl.program_id(0) * (q_ref.shape[1] // HDIM) + local
        k_ext = jnp.concatenate([before_ref[:BLK, cols], k_ref[:, cols]], axis=0)
        v_ext = jnp.concatenate([before_ref[BLK:, cols], v_ref[:, cols]], axis=0)
        window, sink = probabilities(
            q_ref[:, cols], k_ext, sink_k_ref[:, cols], pattern_ref, head, first_block
        )
        from_sink = dot(sink.astype(BF16), sink_v_ref[:, cols], 1, 0)
        for number in range(blocks):
            here = slice(number * BLK, (number + 1) * BLK)
            near = dot(
                window[number].astype(BF16), v_ext[number * BLK : (number + WIN) * BLK], 1, 0
            )
            at = pl.multiple_of(head * HDIM, HDIM)
            out_ref[here, pl.ds(at, HDIM)] = (near + from_sink[here]).astype(BF16)

    @pl.when(pl.program_id(0) == pl.num_programs(0) - 1)
    def _():
        mine = lax.axis_index("dp")
        columns = out_ref.shape[1] // count
        for bit, away_ref in zip(reversed(bits_of(count)), away_refs):
            at = pl.multiple_of(((mine ^ bit) & ~(bit - 1)) * columns, HDIM)
            away_ref[0] = out_ref[:, pl.ds(at, bit * columns)]


def backward_kernel(
    q_ref,
    k_ref,
    v_ref,
    before_ref,
    sink_k_ref,
    sink_v_ref,
    pattern_ref,
    attn_ref,
    grad_ref,
    dq_ref,
    dk_ref,
    dv_ref,
    dbefore_ref,
    kept_ref,
    sent_ref,
):
    rows = q_ref.shape[0]
    blocks = rows // BLK
    first_block = lax.axis_index("ctx") * blocks
    for local in range(q_ref.shape[1] // HDIM):
        cols = slice(local * HDIM, (local + 1) * HDIM)
        head = pl.program_id(0) * (q_ref.shape[1] // HDIM) + local
        q = q_ref[:, cols]
        grad = grad_ref[:, cols]
        k_sink = sink_k_ref[:, cols]
        k_ext = jnp.concatenate([before_ref[:BLK, cols], k_ref[:, cols]], axis=0)
        v_ext = jnp.concatenate([before_ref[BLK:, cols], v_ref[:, cols]], axis=0)
        window, sink = probabilities(q, k_ext, k_sink, pattern_ref, head, first_block)
        delta = jnp.sum(grad.astype(F32) * attn_ref[:, cols].astype(F32), axis=1, keepdims=True)
        dprobs = dot(grad, sink_v_ref[:, cols], 1, 1)
        dscores = (sink * (dprobs - delta)).astype(BF16)
        dq_sink = dot(dscores, k_sink, 1, 0)
        dsink_k = dot(dscores, q, 0, 0) * ROOT
        dsink_v = dot(sink.astype(BF16), grad, 0, 0)
        odd = (lax.axis_index("ctx") & 1) != 0
        kept_ref[:, cols] = jnp.where(odd, dsink_v, dsink_k)
        sent_ref[:, cols] = jnp.where(odd, dsink_k, dsink_v).astype(BF16)
        dk_parts = [None] * (blocks + 1)
        dv_parts = [None] * (blocks + 1)
        for number in range(blocks):
            here = slice(number * BLK, (number + 1) * BLK)
            there = slice(number * BLK, (number + WIN) * BLK)
            dprobs = dot(grad[here], v_ext[there], 1, 1)
            dscores = (window[number] * (dprobs - delta[here])).astype(BF16)
            dq = dot(dscores, k_ext[there], 1, 0)
            dq_ref[here, cols] = ((dq + dq_sink[here]) * ROOT).astype(BF16)
            dk = dot(dscores, q[here], 0, 0) * ROOT
            dv = dot(window[number].astype(BF16), grad[here], 0, 0)
            for part in range(WIN):
                piece = slice(part * BLK, (part + 1) * BLK)
                at = number + part
                dk_parts[at] = dk[piece] if dk_parts[at] is None else dk_parts[at] + dk[piece]
                dv_parts[at] = dv[piece] if dv_parts[at] is None else dv_parts[at] + dv[piece]
        dbefore_ref[:BLK, cols] = dk_parts[0].astype(dbefore_ref.dtype)
        dbefore_ref[BLK:, cols] = dv_parts[0].astype(dbefore_ref.dtype)
        dk_ref[:, cols] = jnp.concatenate(dk_parts[1:], axis=0)
        dv_ref[:, cols] = jnp.concatenate(dv_parts[1:], axis=0)


def head_spec(rows):
    return pl.BlockSpec((rows, HEADS_STEP * HDIM), lambda step: (0, step))


def whole_smem(shape):
    return pl.BlockSpec(shape, lambda *_: (0,) * len(shape), memory_space=pltpu.SMEM)


def attention_specs(rows, pattern):
    return [
        head_spec(rows),
        head_spec(rows),
        head_spec(rows),
        head_spec(2 * BLK),
        head_spec(BLK),
        head_spec(BLK),
        whole_smem(pattern.shape),
    ]


def attention_forward(count, q, k, v, before, sink_k, sink_v, pattern):
    rows, width = q.shape
    away = [bit * width // count for bit in reversed(bits_of(count))]
    return pl.pallas_call(
        functools.partial(forward_kernel, count),
        grid=(width // (HEADS_STEP * HDIM),),
        in_specs=attention_specs(rows, pattern),
        out_specs=[
            pl.BlockSpec((rows, width), lambda step: (0, 0)),
            *(pl.BlockSpec((1, rows, one), lambda step: (0, 0, 0)) for one in away),
        ],
        out_shape=[
            jax.ShapeDtypeStruct((rows, width), BF16),
            *(jax.ShapeDtypeStruct((1, rows, one), BF16) for one in away),
        ],
        name="attention_forward",
    )(q, k, v, before, sink_k, sink_v, pattern)


def attention_backward(q, k, v, before, sink_k, sink_v, pattern, attn, grad):
    rows, width = q.shape
    shape = jax.ShapeDtypeStruct
    return pl.pallas_call(
        backward_kernel,
        grid=(width // (HEADS_STEP * HDIM),),
        in_specs=attention_specs(rows, pattern) + [head_spec(rows), head_spec(rows)],
        out_specs=[
            head_spec(rows),
            head_spec(rows),
            head_spec(rows),
            head_spec(2 * BLK),
            head_spec(BLK),
            head_spec(BLK),
        ],
        out_shape=[
            shape((rows, width), BF16),
            shape((rows, width), F32),
            shape((rows, width), F32),
            shape((2 * BLK, width), BF16),
            shape((BLK, width), F32),
            shape((BLK, width), BF16),
        ],
        name="attention_backward",
    )(q, k, v, before, sink_k, sink_v, pattern, attn, grad)


def grad_attn_kernel(count, *refs):
    cot_ref, pieces, out_ref = refs[0], refs[1:-1], refs[-1]
    mine = lax.axis_index("dp")
    number = 0
    for piece in pieces:
        depth = piece.shape[1]
        for slot in range(piece.shape[0]):
            at = pl.multiple_of((mine ^ order_of(count)[number]) * depth, HDIM)
            out_ref[:, pl.ds(at, depth)] = dot(cot_ref[...], piece[slot], 1, 1).astype(BF16)
            number += 1


def projected_kernel(count, *refs):
    attn_ref, pieces, out_ref = refs[0], refs[1:-1], refs[-1]
    mine = lax.axis_index("dp")
    total, number = None, 0
    for piece in pieces:
        depth = piece.shape[1]
        for slot in range(piece.shape[0]):
            at = pl.multiple_of((mine ^ order_of(count)[number]) * depth, HDIM)
            term = dot(attn_ref[:, pl.ds(at, depth)], piece[slot], 1, 0)
            total = term if total is None else total + term
            number += 1
    out_ref[...] = total.astype(BF16)


def weight_grad_kernel(scale, pairs, *refs):
    lefts, rights = refs[:pairs], refs[pairs : 2 * pairs]
    keep_ref, away_ref, left_scr = refs[2 * pairs :]
    mine = lax.axis_index("dp")
    features = left_scr.shape[0]
    rows = lefts[0].shape[-2]

    @pl.when(pl.program_id(0) == 0)
    def _():
        number = 0
        for left in lefts:
            shared = left.shape[-1] // features
            at = pl.multiple_of((mine & (shared - 1)) * features, HDIM)
            for slot in range(left.shape[0]):
                left_scr[:, number * rows : (number + 1) * rows] = left[
                    slot, :, pl.ds(at, features)
                ].T
                number += 1

    columns = keep_ref.shape[2]
    upper = (lax.axis_index("ctx") & 1) != 0
    for out_ref, here in ((away_ref, jnp.where(upper, 0, columns)), (keep_ref, jnp.where(upper, columns, 0))):
        here = pl.multiple_of(here, HDIM)
        right = jnp.concatenate(
            [one[slot, :, pl.ds(here, columns)] for one in rights for slot in range(one.shape[0])],
            axis=0,
        )
        out_ref[0] = (dot(left_scr[...], right, 1, 0) * scale).astype(out_ref.dtype)


def plain_weight_grad_kernel(scale, pairs, *refs):
    lefts, rights, out_ref = refs[:pairs], refs[pairs : 2 * pairs], refs[-1]
    mine = lax.axis_index("dp")
    features = out_ref.shape[1]
    total = None
    for left, right in zip(lefts, rights):
        at = pl.multiple_of((mine & (left.shape[-1] // features - 1)) * features, HDIM)
        for slot in range(left.shape[0]):
            term = dot(left[slot, :, pl.ds(at, features)], right[slot], 0, 0)
            total = term if total is None else total + term
    out_ref[0] = total * scale


def grad_attn_of(cot, pieces, count):
    rows = cot.shape[0]
    width = count * pieces[0].shape[1]
    return pl.pallas_call(
        functools.partial(grad_attn_kernel, count),
        out_shape=jax.ShapeDtypeStruct((rows, width), BF16),
        name="grad_attn",
    )(cot, *pieces)


def projected_of(attn, pieces, count):
    return pl.pallas_call(
        functools.partial(projected_kernel, count),
        out_shape=jax.ShapeDtypeStruct((attn.shape[0], pieces[0].shape[2]), BF16),
        name="projected",
    )(attn, *pieces)


def weight_grad_of(attn_pieces, cot_pieces, scale, document_count, count):
    features = attn_pieces[0].shape[2] // document_count
    wanted = cot_pieces[0].shape[2] // count
    if wanted % HDIM:
        return plain_weight_grad_of(attn_pieces, cot_pieces, scale, document_count, count)
    rows = attn_pieces[0].shape[1]
    places = len(bits_of(count)) - 1

    def reversed_bits(step):
        return sum(((step >> place) & 1) << (places - 1 - place) for place in range(places))

    out = pl.BlockSpec((1, features, wanted), lambda step: (reversed_bits(step), 0, 0))
    return pl.pallas_call(
        functools.partial(weight_grad_kernel, scale, len(attn_pieces)),
        grid=(count // 2,),
        in_specs=[pl.BlockSpec(a.shape, lambda step: (0, 0, 0)) for a in attn_pieces]
        + [pl.BlockSpec(c.shape[:2] + (2 * wanted,), lambda step: (0, 0, step)) for c in cot_pieces],
        out_specs=[out, out],
        out_shape=[
            jax.ShapeDtypeStruct((count // 2, features, wanted), F32),
            jax.ShapeDtypeStruct((count // 2, features, wanted), BF16),
        ],
        scratch_shapes=[pltpu.VMEM((features, document_count * rows), BF16)],
        name="weight_grad",
    )(*attn_pieces, *cot_pieces)


def plain_weight_grad_of(attn_pieces, cot_pieces, scale, document_count, count):
    features = attn_pieces[0].shape[2] // document_count
    wanted = cot_pieces[0].shape[2] // count
    columns = HDIM
    chunks = cot_pieces[0].shape[2] // columns
    terms = pl.pallas_call(
        functools.partial(plain_weight_grad_kernel, scale, len(attn_pieces)),
        grid=(chunks,),
        in_specs=[pl.BlockSpec(a.shape, lambda step: (0, 0, 0)) for a in attn_pieces]
        + [pl.BlockSpec(c.shape[:2] + (columns,), lambda step: (0, 0, step)) for c in cot_pieces],
        out_specs=pl.BlockSpec((1, features, columns), lambda step: (step, 0, 0)),
        out_shape=jax.ShapeDtypeStruct((chunks, features, columns), F32),
        name="weight_grad",
    )(*attn_pieces, *cot_pieces)
    terms = terms.reshape(chunks, features, columns // wanted, wanted)
    places = len(bits_of(count))
    terms = jnp.swapaxes(terms, 1, 2).reshape((2,) * places + (features, wanted))
    terms = terms.transpose(tuple(reversed(range(places))) + (places, places + 1))
    terms = terms.reshape(2, count // 2, features, wanted)
    here = lax.axis_index("ctx") & 1
    keep = lax.dynamic_index_in_dim(terms, here, 0, keepdims=False)
    return keep, lax.dynamic_index_in_dim(terms, 1 - here, 0, keepdims=False).astype(BF16)


def joined_kernel(dk_ref, dv_ref, later_ref, out_k_ref, out_v_ref):
    rows = dk_ref.shape[0]
    for own, out, at in ((dk_ref, out_k_ref, 0), (dv_ref, out_v_ref, BLK)):
        out[: rows - BLK] = own[: rows - BLK].astype(BF16)
        out[rows - BLK :] = (own[rows - BLK :] + later_ref[at : at + BLK].astype(F32)).astype(BF16)


def joined(dk, dv, later):
    shape = jax.ShapeDtypeStruct(dk.shape, BF16)
    return pl.pallas_call(joined_kernel, out_shape=[shape, shape], name="joined")(dk, dv, later)


def finish_kernel(part_k_ref, part_v_ref, own_k_ref, own_v_ref, total_ref, got_ref, out_k_ref, out_v_ref):
    del part_k_ref, part_v_ref
    first = lax.axis_index("ctx") == 0
    out_k_ref[...] = (own_k_ref[...] + jnp.where(first, total_ref[...], 0.0)).astype(BF16)
    out_v_ref[...] = (own_v_ref[...] + jnp.where(first, got_ref[...].astype(F32), 0.0)).astype(BF16)


def finish(part_k, part_v, own_k, own_v, total, got):
    width = own_k.shape[1]
    block = pl.BlockSpec((BLK, width), lambda step: (0, 0))
    whole = pl.BlockSpec(memory_space=pl.ANY)
    shape = jax.ShapeDtypeStruct(part_k.shape, BF16)
    return pl.pallas_call(
        finish_kernel,
        grid=(1,),
        in_specs=[whole, whole, block, block, block, block],
        out_specs=[block, block],
        out_shape=[shape, shape],
        input_output_aliases={0: 0, 1: 1},
        name="finish",
    )(part_k, part_v, own_k, own_v, total, got)


def bits_of(count):
    return [1 << place for place in range(count.bit_length() - 1)]


def order_of(count):
    order = [0]
    for bit in reversed(bits_of(count)):
        order += [one ^ bit for one in order]
    return order


def swap(value, axis, count, bit):
    return lax.ppermute(value, axis, [(one, one ^ bit) for one in range(count)])


def gather_pieces(value, axis, count, away=None):
    pieces = [value[None]]
    for place, bit in enumerate(reversed(bits_of(count))):
        got = []
        for number, one in enumerate(pieces):
            got.append(swap(away[place] if away and not number else one, axis, count, bit))
        pieces += got
    return pieces


def spread_first(value, axis, count, order):
    mine = lax.axis_index(axis)
    covered = 0
    for bit in order:
        pairs = [(one, one | bit) for one in range(count) if one & ~covered == 0]
        got = lax.ppermute(value, axis, pairs)
        value = jnp.where((mine & bit) != 0, got, value)
        covered |= bit
    return value


def sum_to_first(kept, sent, axis, count):
    bits = bits_of(count)
    kept = kept + swap(sent, axis, count, 1).astype(F32)
    done = 0
    for bit in bits[1:]:
        pairs = [(one, one ^ bit) for one in range(count) if one & bit and one & done == 0]
        kept = kept + lax.ppermute(kept.astype(BF16), axis, pairs).astype(F32)
        done |= bit
    return kept, lax.ppermute(kept.astype(BF16), axis, [(1, 0)])


def sum_scatter(keep, away, axis, count):
    mine = lax.axis_index(axis)
    bits = bits_of(count)
    keep = keep.reshape((2,) * (len(bits) - 1) + keep.shape[1:])
    away = away.reshape(keep.shape)
    for place, bit in enumerate(bits):
        if place:
            here = jnp.where((mine & bit) != 0, 1, 0)
            away = lax.dynamic_index_in_dim(keep, 1 - here, 0, keepdims=False).astype(BF16)
            keep = lax.dynamic_index_in_dim(keep, here, 0, keepdims=False)
        keep = keep + swap(away, axis, count, bit).astype(F32)
    return keep


def body(context_count, document_count, queries, keys, values, cotangent, proj_weight, pattern):
    q, k, v, cot = queries[0], keys[0], values[0], cotangent[0]
    rows, _ = q.shape
    bits = bits_of(context_count)
    far_first = bits[:0:-1]

    last = jnp.concatenate([k[rows - BLK :], v[rows - BLK :]], axis=0)
    before = lax.ppermute(last, "ctx", [(one, one + 1) for one in range(context_count - 1)])
    sink_k = spread_first(k[:BLK], "ctx", context_count, bits[:1] + far_first)
    sink_v = spread_first(v[:BLK], "ctx", context_count, far_first + bits[:1])
    weights = gather_pieces(proj_weight, "dp", document_count)
    cots = gather_pieces(cot, "dp", document_count)
    grad_attn = grad_attn_of(cot, weights, document_count)
    attn, *away = attention_forward(
        document_count, q, k, v, before, sink_k, sink_v, pattern
    )
    attns = gather_pieces(attn, "dp", document_count, away)
    dq, dk, dv, dbefore, kept, sent = attention_backward(
        q, k, v, before, sink_k, sink_v, pattern, attn, grad_attn
    )
    later = lax.ppermute(dbefore, "ctx", [(one + 1, one) for one in range(context_count - 1)])
    total, got = sum_to_first(kept, sent, "ctx", context_count)
    projected = projected_of(attn, weights, document_count)
    scale = float(rows * context_count * document_count) ** (-0.5)
    keep, send = weight_grad_of(attns, cots, scale, document_count, context_count)
    grad_proj = sum_scatter(keep, send, "ctx", context_count)
    grad_k, grad_v = joined(dk, dv, later)
    grad_k, grad_v = finish(grad_k, grad_v, dk, dv, total, got)
    return projected[None], dq[None], grad_k[None], grad_v[None], grad_proj


def solution(mesh):
    sizes = mesh.shape["ctx"], mesh.shape["dp"]
    return jax.shard_map(
        functools.partial(body, *sizes),
        mesh=mesh,
        in_specs=(
            P("dp", "ctx", None),
            P("dp", "ctx", None),
            P("dp", "ctx", None),
            P("dp", "ctx", None),
            P("dp", None),
            P("dp", None, None, None),
        ),
        out_specs=(
            P("dp", "ctx", None),
            P("dp", "ctx", None),
            P("dp", "ctx", None),
            P("dp", "ctx", None),
            P("dp", "ctx"),
        ),
        check_vma=False,
    )
```

```python
import functools
import math

import jax
import jax.numpy as jnp
from jax import lax
from jax.experimental import pallas as pl
from jax.experimental.pallas import tpu as pltpu
from jax.sharding import PartitionSpec as P


HDIM = 128
BLK = 128

WIN = 2
HEADS_STEP = 4

ROWS_STEP = 64
LOG2_E = math.log2(math.e)
MASKED = -1e30
ROOT = HDIM ** (-0.5)
F32 = jnp.float32
BF16 = jnp.bfloat16


def dot(left, right, left_dim, right_dim):
    return lax.dot_general(
        left, right, (((left_dim,), (right_dim,)), ((), ())), preferred_element_type=F32
    )


def sink_of(kept, got, bit):
    return jnp.where((lax.axis_index("ctx") & bit) != 0, got, kept)


def softmax_rows(scores_ref, at, pattern_ref, head, block, first_row):
    scores = scores_ref[at]
    shape = (scores.shape[0], BLK)
    causal = lax.broadcasted_iota(jnp.int32, shape, 1) <= (
        lax.broadcasted_iota(jnp.int32, shape, 0) + first_row
    )
    reached = jnp.logical_and(pattern_ref[0, head, block, 1] == 1, block >= 2)
    before = jnp.where(reached, scores[:, :BLK], MASKED)
    own = jnp.where(jnp.logical_and(causal, block >= 1), scores[:, BLK : 2 * BLK], MASKED)
    first = jnp.where(jnp.logical_or(causal, block >= 1), scores[:, 2 * BLK :], MASKED)
    top = jnp.max(jnp.maximum(jnp.maximum(before, own), first), axis=1, keepdims=True)
    parts = [jnp.exp2((one - top) * (ROOT * LOG2_E)) for one in (before, own, first)]
    total = jnp.sum(parts[0] + parts[1] + parts[2], axis=1, keepdims=True)
    return parts, top, 1.0 / total


def forward_kernel(
    count,
    last_bits,
    q_ref,
    k_ref,
    v_ref,
    before_ref,
    kept_k_ref,
    kept_v_ref,
    got_k_ref,
    got_v_ref,
    pattern_ref,
    grad_ref,
    out_ref,
    probs_ref,
    stats_ref,
    *rest,
):
    away_refs, (scores_ref, rounded_ref) = rest[:-2], rest[-2:]
    rows = q_ref.shape[0]
    blocks = rows // BLK
    heads = q_ref.shape[1] // HDIM
    total_heads = out_ref.shape[1] // HDIM
    first_block = lax.axis_index("ctx") * blocks
    first_head = pl.program_id(0) * heads

    @pl.when(pl.program_id(0) == 0)
    def _():
        stats_ref[...] = jnp.zeros_like(stats_ref)

    for local in range(heads):
        cols = slice(local * HDIM, (local + 1) * HDIM)
        k_ext = jnp.concatenate([before_ref[:BLK, cols], k_ref[:, cols]], axis=0)
        k_sink = sink_of(kept_k_ref[:, cols], got_k_ref[:, cols], last_bits[0])
        scores_ref[local, :, 2 * BLK :] = dot(q_ref[:, cols], k_sink, 1, 1)
        for number in range(blocks):
            here = slice(number * BLK, (number + 1) * BLK)
            there = slice(number * BLK, (number + WIN) * BLK)
            scores_ref[local, here, : 2 * BLK] = dot(q_ref[here, cols], k_ext[there], 1, 1)
    lane = lax.broadcasted_iota(jnp.int32, (ROWS_STEP, BLK), 1)
    for local in range(heads):
        cols = slice(local * HDIM, (local + 1) * HDIM)
        head = first_head + local
        for row in range(0, rows, ROWS_STEP):
            at = slice(row, row + ROWS_STEP)
            parts, top, inverse = softmax_rows(
                scores_ref.at[local], at, pattern_ref, head, first_block + row // BLK, row % BLK
            )
            for place, part in enumerate(parts):
                there = slice(place * BLK, (place + 1) * BLK)
                part = part * inverse
                probs_ref[local, at, there] = part
                rounded_ref[local, at, there] = part.astype(BF16)
            if row < BLK:
                stats = stats_ref[at]
                stats = jnp.where(lane == head, top, stats)
                stats_ref[at] = jnp.where(lane == head + total_heads, inverse, stats)
    for local in range(heads):
        cols = slice(local * HDIM, (local + 1) * HDIM)
        head = first_head + local
        v_ext = jnp.concatenate([before_ref[BLK:, cols], v_ref[:, cols]], axis=0)
        v_sink = sink_of(kept_v_ref[:, cols], got_v_ref[:, cols], last_bits[1])
        from_sink = dot(rounded_ref[local, :, 2 * BLK :], v_sink, 1, 0)
        for number in range(blocks):
            here = slice(number * BLK, (number + 1) * BLK)
            there = slice(number * BLK, (number + WIN) * BLK)
            near = dot(rounded_ref[local, here, : 2 * BLK], v_ext[there], 1, 0)
            attended = (near + from_sink[here]).astype(BF16)
            out_ref[here, pl.ds(pl.multiple_of(head * HDIM, HDIM), HDIM)] = attended
            if number == 0:
                delta = jnp.sum(
                    grad_ref[:BLK, cols].astype(F32) * attended.astype(F32), axis=1, keepdims=True
                )
                wide = lax.broadcasted_iota(jnp.int32, (BLK, BLK), 1)
                stats_ref[...] = jnp.where(wide == head + 2 * total_heads, delta, stats_ref[...])

    @pl.when(pl.program_id(0) == pl.num_programs(0) - 1)
    def _():
        mine = lax.axis_index("dp")
        columns = out_ref.shape[1] // count
        for bit, away_ref in zip(reversed(bits_of(count)), away_refs):
            at = pl.multiple_of(((mine ^ bit) & ~(bit - 1)) * columns, HDIM)
            away_ref[0] = out_ref[:, pl.ds(at, bit * columns)]


def backward_kernel(
    last_bits,
    q_ref,
    k_ref,
    v_ref,
    before_ref,
    kept_k_ref,
    kept_v_ref,
    got_k_ref,
    got_v_ref,
    probs_ref,
    attn_ref,
    grad_ref,
    dq_ref,
    dk_ref,
    dv_ref,
    kept_ref,
    sent_ref,
    dprobs_ref,
    dscores_ref,
    rounded_ref,
):
    rows = q_ref.shape[0]
    blocks = rows // BLK
    heads = q_ref.shape[1] // HDIM
    for local in range(heads):
        cols = slice(local * HDIM, (local + 1) * HDIM)
        v_ext = jnp.concatenate([before_ref[BLK:, cols], v_ref[:, cols]], axis=0)
        v_sink = sink_of(kept_v_ref[:, cols], got_v_ref[:, cols], last_bits[1])
        dprobs_ref[local, :, 2 * BLK :] = dot(grad_ref[:, cols], v_sink, 1, 1)
        for number in range(blocks):
            here = slice(number * BLK, (number + 1) * BLK)
            there = slice(number * BLK, (number + WIN) * BLK)
            dprobs_ref[local, here, : 2 * BLK] = dot(grad_ref[here, cols], v_ext[there], 1, 1)
    for local in range(heads):
        cols = slice(local * HDIM, (local + 1) * HDIM)
        for row in range(0, rows, ROWS_STEP):
            at = slice(row, row + ROWS_STEP)
            delta = jnp.sum(
                grad_ref[at, cols].astype(F32) * attn_ref[at, cols].astype(F32),
                axis=1,
                keepdims=True,
            )
            probs = probs_ref[local, at]
            dscores_ref[local, at] = (probs * (dprobs_ref[local, at] - delta)).astype(BF16)
            rounded_ref[local, at] = probs.astype(BF16)
    odd = (lax.axis_index("ctx") & 1) != 0
    for local in range(heads):
        cols = slice(local * HDIM, (local + 1) * HDIM)
        q = q_ref[:, cols]
        grad = grad_ref[:, cols]
        k_ext = jnp.concatenate([before_ref[:BLK, cols], k_ref[:, cols]], axis=0)
        k_sink = sink_of(kept_k_ref[:, cols], got_k_ref[:, cols], last_bits[0])
        dq_sink = dot(dscores_ref[local, :, 2 * BLK :], k_sink, 1, 0)
        for number in range(blocks):
            here = slice(number * BLK, (number + 1) * BLK)
            there = slice(number * BLK, (number + WIN) * BLK)
            dq = dot(dscores_ref[local, here, : 2 * BLK], k_ext[there], 1, 0)
            dq_ref[here, cols] = ((dq + dq_sink[here]) * ROOT).astype(BF16)
        dsink_k = dot(dscores_ref[local, :, 2 * BLK :], q, 0, 0) * ROOT
        dsink_v = dot(rounded_ref[local, :, 2 * BLK :], grad, 0, 0)
        kept_ref[:, cols] = jnp.where(odd, dsink_v, dsink_k)
        sent_ref[:, cols] = jnp.where(odd, dsink_k, dsink_v).astype(BF16)
        for number in range(blocks):
            here = slice(number * BLK, (number + 1) * BLK)
            own = slice(BLK, 2 * BLK)
            dk = dot(dscores_ref[local, here, own], q[here], 0, 0)
            dv = dot(rounded_ref[local, here, own], grad[here], 0, 0)
            if number + 1 < blocks:
                above = slice((number + 1) * BLK, (number + 2) * BLK)
                dk += dot(dscores_ref[local, above, :BLK], q[above], 0, 0)
                dv += dot(rounded_ref[local, above, :BLK], grad[above], 0, 0)
            dk_ref[here, cols] = dk * ROOT
            dv_ref[here, cols] = dv


def next_kernel(
    k_ref, v_ref, next_ref, stats_ref, pattern_ref, dk_ref, dv_ref, out_k_ref, out_v_ref
):
    rows = k_ref.shape[0]
    last = slice(rows - BLK, rows)
    heads = k_ref.shape[1] // HDIM
    total_heads = pl.num_programs(0) * heads
    block = (lax.axis_index("ctx") + 1) * (rows // BLK)
    inside = jnp.minimum(block, pattern_ref.shape[2] - 1)
    lane = lax.broadcasted_iota(jnp.int32, (BLK, BLK), 1)
    stats = stats_ref[...]

    def column(index):
        return jnp.sum(jnp.where(lane == index, stats, 0.0), axis=1, keepdims=True)

    for local in range(heads):
        cols = slice(local * HDIM, (local + 1) * HDIM)
        head = pl.program_id(0) * heads + local
        top, inverse, delta = (column(head + kind * total_heads) for kind in range(3))
        q, grad = next_ref[:BLK, cols], next_ref[BLK:, cols]
        scores = dot(q, k_ref[last, cols], 1, 1)
        reached = jnp.logical_and(pattern_ref[0, head, inside, 1] == 1, block >= 2)
        probs = jnp.exp2((scores - top) * (ROOT * LOG2_E)) * inverse
        probs = jnp.where(reached, probs, 0.0)
        dprobs = dot(grad, v_ref[last, cols], 1, 1)
        dscores = (probs * (dprobs - delta)).astype(BF16)
        dk = dk_ref[last, cols] + dot(dscores, q, 0, 0) * ROOT
        dv = dv_ref[last, cols] + dot(probs.astype(BF16), grad, 0, 0)
        out_k_ref[last, cols] = dk.astype(BF16)
        out_v_ref[last, cols] = dv.astype(BF16)
    out_k_ref[: rows - BLK] = dk_ref[: rows - BLK].astype(BF16)
    out_v_ref[: rows - BLK] = dv_ref[: rows - BLK].astype(BF16)


def head_spec(rows):
    return pl.BlockSpec((rows, HEADS_STEP * HDIM), lambda step: (0, step))


def whole_smem(shape):
    return pl.BlockSpec(shape, lambda *_: (0,) * len(shape), memory_space=pltpu.SMEM)


def attention_specs(rows):
    return [
        head_spec(rows),
        head_spec(rows),
        head_spec(rows),
        head_spec(2 * BLK),
        head_spec(BLK),
        head_spec(BLK),
        head_spec(BLK),
        head_spec(BLK),
    ]


def probs_spec(rows):
    return pl.BlockSpec((HEADS_STEP, rows, (WIN + 1) * BLK), lambda step: (step, 0, 0))


def attention_forward(count, last_bits, q, k, v, before, sinks, pattern, grad):
    rows, width = q.shape
    heads = width // HDIM
    away = [bit * width // count for bit in reversed(bits_of(count))]
    shape = jax.ShapeDtypeStruct
    return pl.pallas_call(
        functools.partial(forward_kernel, count, last_bits),
        grid=(heads // HEADS_STEP,),
        in_specs=attention_specs(rows) + [whole_smem(pattern.shape), head_spec(rows)],
        out_specs=[
            pl.BlockSpec((rows, width), lambda step: (0, 0)),
            probs_spec(rows),
            pl.BlockSpec((BLK, BLK), lambda step: (0, 0)),
            *(pl.BlockSpec((1, rows, one), lambda step: (0, 0, 0)) for one in away),
        ],
        out_shape=[
            shape((rows, width), BF16),
            shape((heads, rows, (WIN + 1) * BLK), F32),
            shape((BLK, BLK), F32),
            *(shape((1, rows, one), BF16) for one in away),
        ],
        scratch_shapes=[
            pltpu.VMEM((HEADS_STEP, rows, (WIN + 1) * BLK), F32),
            pltpu.VMEM((HEADS_STEP, rows, (WIN + 1) * BLK), BF16),
        ],
        name="attention_forward",
    )(q, k, v, before, *sinks, pattern, grad)


def attention_backward(last_bits, q, k, v, before, sinks, probs, attn, grad):
    rows, width = q.shape
    shape = jax.ShapeDtypeStruct
    scratch = (HEADS_STEP, rows, (WIN + 1) * BLK)
    return pl.pallas_call(
        functools.partial(backward_kernel, last_bits),
        grid=(width // (HEADS_STEP * HDIM),),
        in_specs=attention_specs(rows) + [probs_spec(rows), head_spec(rows), head_spec(rows)],
        out_specs=[
            head_spec(rows),
            head_spec(rows),
            head_spec(rows),
            head_spec(BLK),
            head_spec(BLK),
        ],
        out_shape=[
            shape((rows, width), BF16),
            shape((rows, width), F32),
            shape((rows, width), F32),
            shape((BLK, width), F32),
            shape((BLK, width), BF16),
        ],
        scratch_shapes=[
            pltpu.VMEM(scratch, F32),
            pltpu.VMEM(scratch, BF16),
            pltpu.VMEM(scratch, BF16),
        ],
        name="attention_backward",
    )(q, k, v, before, *sinks, probs, attn, grad)


def next_backward(k, v, following, stats, pattern, dk, dv):
    rows, width = k.shape
    shape = jax.ShapeDtypeStruct((rows, width), BF16)
    return pl.pallas_call(
        next_kernel,
        grid=(width // (HEADS_STEP * HDIM),),
        in_specs=[
            head_spec(rows),
            head_spec(rows),
            head_spec(2 * BLK),
            pl.BlockSpec((BLK, BLK), lambda step: (0, 0)),
            whole_smem(pattern.shape),
            head_spec(rows),
            head_spec(rows),
        ],
        out_specs=[head_spec(rows), head_spec(rows)],
        out_shape=[shape, shape],
        name="next_backward",
    )(k, v, following, stats, pattern, dk, dv)


def grad_attn_kernel(count, *refs):
    cot_ref, q_ref, pieces, out_ref, back_ref = refs[0], refs[1], refs[2:-2], refs[-2], refs[-1]
    mine = lax.axis_index("dp")
    number = 0
    for piece in pieces:
        depth = piece.shape[1]
        for slot in range(piece.shape[0]):
            at = pl.multiple_of((mine ^ order_of(count)[number]) * depth, HDIM)
            out_ref[:, pl.ds(at, depth)] = dot(cot_ref[...], piece[slot], 1, 1).astype(BF16)
            number += 1
    back_ref[:BLK] = q_ref[:BLK]
    back_ref[BLK:] = out_ref[:BLK]


def projected_kernel(count, *refs):
    attn_ref, pieces, out_ref = refs[0], refs[1:-1], refs[-1]
    mine = lax.axis_index("dp")
    total, number = None, 0
    for piece in pieces:
        depth = piece.shape[1]
        for slot in range(piece.shape[0]):
            at = pl.multiple_of((mine ^ order_of(count)[number]) * depth, HDIM)
            term = dot(attn_ref[:, pl.ds(at, depth)], piece[slot], 1, 0)
            total = term if total is None else total + term
            number += 1
    out_ref[...] = total.astype(BF16)


def weight_grad_kernel(scale, pairs, *refs):
    lefts, rights = refs[:pairs], refs[pairs : 2 * pairs]
    keep_ref, away_ref, left_scr = refs[2 * pairs :]
    mine = lax.axis_index("dp")
    features = left_scr.shape[0]
    rows = lefts[0].shape[-2]

    @pl.when(pl.program_id(0) == 0)
    def _():
        number = 0
        for left in lefts:
            shared = left.shape[-1] // features
            at = pl.multiple_of((mine & (shared - 1)) * features, HDIM)
            for slot in range(left.shape[0]):
                left_scr[:, number * rows : (number + 1) * rows] = left[
                    slot, :, pl.ds(at, features)
                ].T
                number += 1

    columns = keep_ref.shape[2]
    upper = (lax.axis_index("ctx") & 1) != 0
    for out_ref, here in ((away_ref, jnp.where(upper, 0, columns)), (keep_ref, jnp.where(upper, columns, 0))):
        here = pl.multiple_of(here, HDIM)
        right = jnp.concatenate(
            [one[slot, :, pl.ds(here, columns)] for one in rights for slot in range(one.shape[0])],
            axis=0,
        )
        out_ref[0] = (dot(left_scr[...], right, 1, 0) * scale).astype(out_ref.dtype)


def plain_weight_grad_kernel(scale, pairs, *refs):
    lefts, rights, out_ref = refs[:pairs], refs[pairs : 2 * pairs], refs[-1]
    mine = lax.axis_index("dp")
    features = out_ref.shape[1]
    total = None
    for left, right in zip(lefts, rights):
        at = pl.multiple_of((mine & (left.shape[-1] // features - 1)) * features, HDIM)
        for slot in range(left.shape[0]):
            term = dot(left[slot, :, pl.ds(at, features)], right[slot], 0, 0)
            total = term if total is None else total + term
    out_ref[0] = total * scale


def grad_attn_of(cot, q, pieces, count):
    rows = cot.shape[0]
    width = count * pieces[0].shape[1]
    return pl.pallas_call(
        functools.partial(grad_attn_kernel, count),
        out_shape=[
            jax.ShapeDtypeStruct((rows, width), BF16),
            jax.ShapeDtypeStruct((2 * BLK, width), BF16),
        ],
        name="grad_attn",
    )(cot, q, *pieces)


def projected_of(attn, pieces, count):
    return pl.pallas_call(
        functools.partial(projected_kernel, count),
        out_shape=jax.ShapeDtypeStruct((attn.shape[0], pieces[0].shape[2]), BF16),
        name="projected",
    )(attn, *pieces)


def weight_grad_of(attn_pieces, cot_pieces, scale, document_count, count):
    features = attn_pieces[0].shape[2] // document_count
    wanted = cot_pieces[0].shape[2] // count
    if wanted % HDIM:
        return plain_weight_grad_of(attn_pieces, cot_pieces, scale, document_count, count)
    rows = attn_pieces[0].shape[1]
    places = len(bits_of(count)) - 1

    def reversed_bits(step):
        return sum(((step >> place) & 1) << (places - 1 - place) for place in range(places))

    out = pl.BlockSpec((1, features, wanted), lambda step: (reversed_bits(step), 0, 0))
    return pl.pallas_call(
        functools.partial(weight_grad_kernel, scale, len(attn_pieces)),
        grid=(count // 2,),
        in_specs=[pl.BlockSpec(a.shape, lambda step: (0, 0, 0)) for a in attn_pieces]
        + [pl.BlockSpec(c.shape[:2] + (2 * wanted,), lambda step: (0, 0, step)) for c in cot_pieces],
        out_specs=[out, out],
        out_shape=[
            jax.ShapeDtypeStruct((count // 2, features, wanted), F32),
            jax.ShapeDtypeStruct((count // 2, features, wanted), BF16),
        ],
        scratch_shapes=[pltpu.VMEM((features, document_count * rows), BF16)],
        name="weight_grad",
    )(*attn_pieces, *cot_pieces)


def plain_weight_grad_of(attn_pieces, cot_pieces, scale, document_count, count):
    features = attn_pieces[0].shape[2] // document_count
    wanted = cot_pieces[0].shape[2] // count
    columns = HDIM
    chunks = cot_pieces[0].shape[2] // columns
    terms = pl.pallas_call(
        functools.partial(plain_weight_grad_kernel, scale, len(attn_pieces)),
        grid=(chunks,),
        in_specs=[pl.BlockSpec(a.shape, lambda step: (0, 0, 0)) for a in attn_pieces]
        + [pl.BlockSpec(c.shape[:2] + (columns,), lambda step: (0, 0, step)) for c in cot_pieces],
        out_specs=pl.BlockSpec((1, features, columns), lambda step: (step, 0, 0)),
        out_shape=jax.ShapeDtypeStruct((chunks, features, columns), F32),
        name="weight_grad",
    )(*attn_pieces, *cot_pieces)
    terms = terms.reshape(chunks, features, columns // wanted, wanted)
    places = len(bits_of(count))
    terms = jnp.swapaxes(terms, 1, 2).reshape((2,) * places + (features, wanted))
    terms = terms.transpose(tuple(reversed(range(places))) + (places, places + 1))
    terms = terms.reshape(2, count // 2, features, wanted)
    here = lax.axis_index("ctx") & 1
    keep = lax.dynamic_index_in_dim(terms, here, 0, keepdims=False)
    return keep, lax.dynamic_index_in_dim(terms, 1 - here, 0, keepdims=False).astype(BF16)


def finish_kernel(part_k_ref, part_v_ref, own_k_ref, own_v_ref, total_ref, got_ref, out_k_ref, out_v_ref):
    del part_k_ref, part_v_ref
    first = lax.axis_index("ctx") == 0
    out_k_ref[...] = (own_k_ref[...] + jnp.where(first, total_ref[...], 0.0)).astype(BF16)
    out_v_ref[...] = (own_v_ref[...] + jnp.where(first, got_ref[...].astype(F32), 0.0)).astype(BF16)


def finish(part_k, part_v, own_k, own_v, total, got):
    width = own_k.shape[1]
    block = pl.BlockSpec((BLK, width), lambda step: (0, 0))
    whole = pl.BlockSpec(memory_space=pl.ANY)
    shape = jax.ShapeDtypeStruct(part_k.shape, BF16)
    return pl.pallas_call(
        finish_kernel,
        grid=(1,),
        in_specs=[whole, whole, block, block, block, block],
        out_specs=[block, block],
        out_shape=[shape, shape],
        input_output_aliases={0: 0, 1: 1},
        name="finish",
    )(part_k, part_v, own_k, own_v, total, got)


def bits_of(count):
    return [1 << place for place in range(count.bit_length() - 1)]


def order_of(count):
    order = [0]
    for bit in reversed(bits_of(count)):
        order += [one ^ bit for one in order]
    return order


def swap(value, axis, count, bit):
    return lax.ppermute(value, axis, [(one, one ^ bit) for one in range(count)])


def gather_pieces(value, axis, count, away=None):
    pieces = [value[None]]
    for place, bit in enumerate(reversed(bits_of(count))):
        got = []
        for number, one in enumerate(pieces):
            got.append(swap(away[place] if away and not number else one, axis, count, bit))
        pieces += got
    return pieces


def spread_first(value, axis, count, order):
    mine = lax.axis_index(axis)
    covered = 0
    got = None
    for place, bit in enumerate(order):
        if place:
            value = jnp.where((mine & order[place - 1]) != 0, got, value)
        pairs = [(one, one | bit) for one in range(count) if one & ~covered == 0]
        got = lax.ppermute(value, axis, pairs)
        covered |= bit
    return value, got


def sum_to_first(kept, sent, axis, count):
    bits = bits_of(count)
    kept = kept + swap(sent, axis, count, 1).astype(F32)
    done = 0
    for bit in bits[1:]:
        pairs = [(one, one ^ bit) for one in range(count) if one & bit and one & done == 0]
        kept = kept + lax.ppermute(kept.astype(BF16), axis, pairs).astype(F32)
        done |= bit
    return kept, lax.ppermute(kept.astype(BF16), axis, [(1, 0)])


def sum_scatter(keep, away, axis, count):
    mine = lax.axis_index(axis)
    bits = bits_of(count)
    keep = keep.reshape((2,) * (len(bits) - 1) + keep.shape[1:])
    away = away.reshape(keep.shape)
    for place, bit in enumerate(bits):
        if place:
            here = jnp.where((mine & bit) != 0, 1, 0)
            away = lax.dynamic_index_in_dim(keep, 1 - here, 0, keepdims=False).astype(BF16)
            keep = lax.dynamic_index_in_dim(keep, here, 0, keepdims=False)
        keep = keep + swap(away, axis, count, bit).astype(F32)
    return keep


def body(context_count, document_count, queries, keys, values, cotangent, proj_weight, pattern):
    q, k, v, cot = queries[0], keys[0], values[0], cotangent[0]
    rows, _ = q.shape
    bits = bits_of(context_count)
    far_first = bits[:0:-1]

    last = jnp.concatenate([k[rows - BLK :], v[rows - BLK :]], axis=0)
    before = lax.ppermute(last, "ctx", [(one, one + 1) for one in range(context_count - 1)])
    order_k, order_v = bits[:1] + far_first, far_first + bits[:1]
    last_bits = order_k[-1], order_v[-1]
    kept_k, got_k = spread_first(k[:BLK], "ctx", context_count, order_k)
    kept_v, got_v = spread_first(v[:BLK], "ctx", context_count, order_v)
    sinks = kept_k, kept_v, got_k, got_v
    weights = gather_pieces(proj_weight, "dp", document_count)
    cots = gather_pieces(cot, "dp", document_count)
    back = [(one + 1, one) for one in range(context_count - 1)]
    grad_attn, following = grad_attn_of(cot, q, weights, document_count)
    following = lax.ppermute(following, "ctx", back)
    attn, probs, stats, *away = attention_forward(document_count, last_bits, q, k, v, before, sinks, pattern, grad_attn)
    attns = gather_pieces(attn, "dp", document_count, away)
    stats = lax.ppermute(stats, "ctx", back)
    dq, dk, dv, kept, sent = attention_backward(
        last_bits, q, k, v, before, sinks, probs, attn, grad_attn
    )
    total, got = sum_to_first(kept, sent, "ctx", context_count)
    projected = projected_of(attn, weights, document_count)
    scale = float(rows * context_count * document_count) ** (-0.5)
    keep, send = weight_grad_of(attns, cots, scale, document_count, context_count)
    grad_proj = sum_scatter(keep, send, "ctx", context_count)
    grad_k, grad_v = next_backward(k, v, following, stats, pattern, dk, dv)
    grad_k, grad_v = finish(grad_k, grad_v, dk, dv, total, got)
    return projected[None], dq[None], grad_k[None], grad_v[None], grad_proj


def solution(mesh):
    sizes = mesh.shape["ctx"], mesh.shape["dp"]
    return jax.shard_map(
        functools.partial(body, *sizes),
        mesh=mesh,
        in_specs=(
            P("dp", "ctx", None),
            P("dp", "ctx", None),
            P("dp", "ctx", None),
            P("dp", "ctx", None),
            P("dp", None),
            P("dp", None, None, None),
        ),
        out_specs=(
            P("dp", "ctx", None),
            P("dp", "ctx", None),
            P("dp", "ctx", None),
            P("dp", "ctx", None),
            P("dp", "ctx"),
        ),
        check_vma=False,
    )
```

```python
import functools
import math

import jax
import jax.numpy as jnp
from jax import lax
from jax.experimental import pallas as pl
from jax.experimental.pallas import tpu as pltpu
from jax.sharding import PartitionSpec as P


HDIM = 128
BLK = 128

WIN = 2
HEADS_STEP = 4

ROWS_STEP = 64
LOG2_E = math.log2(math.e)
MASKED = -1e30
ROOT = HDIM ** (-0.5)
F32 = jnp.float32
BF16 = jnp.bfloat16


def dot(left, right, left_dim, right_dim):
    return lax.dot_general(
        left, right, (((left_dim,), (right_dim,)), ((), ())), preferred_element_type=F32
    )


def sink_of(kept, got, bit):
    return jnp.where((lax.axis_index("ctx") & bit) != 0, got, kept)


def softmax_rows(scores_ref, at, pattern_ref, head, block, first_row):
    scores = scores_ref[at]
    shape = (scores.shape[0], BLK)
    causal = lax.broadcasted_iota(jnp.int32, shape, 1) <= (
        lax.broadcasted_iota(jnp.int32, shape, 0) + first_row
    )
    reached = jnp.logical_and(pattern_ref[0, head, block, 1] == 1, block >= 2)
    before = jnp.where(reached, scores[:, :BLK], MASKED)
    own = jnp.where(jnp.logical_and(causal, block >= 1), scores[:, BLK : 2 * BLK], MASKED)
    first = jnp.where(jnp.logical_or(causal, block >= 1), scores[:, 2 * BLK :], MASKED)
    top = jnp.max(jnp.maximum(jnp.maximum(before, own), first), axis=1, keepdims=True)
    parts = [jnp.exp2((one - top) * (ROOT * LOG2_E)) for one in (before, own, first)]
    total = jnp.sum(parts[0] + parts[1] + parts[2], axis=1, keepdims=True)
    return parts, top, 1.0 / total


def forward_kernel(
    count,
    last_bits,
    q_ref,
    k_ref,
    v_ref,
    before_ref,
    kept_k_ref,
    kept_v_ref,
    got_k_ref,
    got_v_ref,
    pattern_ref,
    grad_ref,
    out_ref,
    probs_ref,
    stats_ref,
    *rest,
):
    away_refs, (scores_ref, rounded_ref) = rest[:-2], rest[-2:]
    rows = q_ref.shape[0]
    blocks = rows // BLK
    heads = q_ref.shape[1] // HDIM
    total_heads = out_ref.shape[1] // HDIM
    first_block = lax.axis_index("ctx") * blocks
    first_head = pl.program_id(0) * heads

    @pl.when(pl.program_id(0) == 0)
    def _():
        stats_ref[...] = jnp.zeros_like(stats_ref)

    for local in range(heads):
        cols = slice(local * HDIM, (local + 1) * HDIM)
        k_ext = jnp.concatenate([before_ref[:BLK, cols], k_ref[:, cols]], axis=0)
        k_sink = sink_of(kept_k_ref[:, cols], got_k_ref[:, cols], last_bits[0])
        scores_ref[local, :, 2 * BLK :] = dot(q_ref[:, cols], k_sink, 1, 1)
        for number in range(blocks):
            here = slice(number * BLK, (number + 1) * BLK)
            there = slice(number * BLK, (number + WIN) * BLK)
            scores_ref[local, here, : 2 * BLK] = dot(q_ref[here, cols], k_ext[there], 1, 1)
    lane = lax.broadcasted_iota(jnp.int32, (ROWS_STEP, BLK), 1)
    for local in range(heads):
        cols = slice(local * HDIM, (local + 1) * HDIM)
        head = first_head + local
        for row in range(0, rows, ROWS_STEP):
            at = slice(row, row + ROWS_STEP)
            parts, top, inverse = softmax_rows(
                scores_ref.at[local], at, pattern_ref, head, first_block + row // BLK, row % BLK
            )
            for place, part in enumerate(parts):
                there = slice(place * BLK, (place + 1) * BLK)
                part = part * inverse
                probs_ref[local, at, there] = part
                rounded_ref[local, at, there] = part.astype(BF16)
            if row < BLK:
                stats = stats_ref[at]
                stats = jnp.where(lane == head, top, stats)
                stats_ref[at] = jnp.where(lane == head + total_heads, inverse, stats)
    for local in range(heads):
        cols = slice(local * HDIM, (local + 1) * HDIM)
        head = first_head + local
        v_ext = jnp.concatenate([before_ref[BLK:, cols], v_ref[:, cols]], axis=0)
        v_sink = sink_of(kept_v_ref[:, cols], got_v_ref[:, cols], last_bits[1])
        from_sink = dot(rounded_ref[local, :, 2 * BLK :], v_sink, 1, 0)
        for number in range(blocks):
            here = slice(number * BLK, (number + 1) * BLK)
            there = slice(number * BLK, (number + WIN) * BLK)
            near = dot(rounded_ref[local, here, : 2 * BLK], v_ext[there], 1, 0)
            attended = (near + from_sink[here]).astype(BF16)
            out_ref[here, pl.ds(pl.multiple_of(head * HDIM, HDIM), HDIM)] = attended
            if number == 0:
                delta = jnp.sum(
                    grad_ref[:BLK, cols].astype(F32) * attended.astype(F32), axis=1, keepdims=True
                )
                wide = lax.broadcasted_iota(jnp.int32, (BLK, BLK), 1)
                stats_ref[...] = jnp.where(wide == head + 2 * total_heads, delta, stats_ref[...])

    @pl.when(pl.program_id(0) == pl.num_programs(0) - 1)
    def _():
        mine = lax.axis_index("dp")
        columns = out_ref.shape[1] // count
        for bit, away_ref in zip(reversed(bits_of(count)), away_refs):
            at = pl.multiple_of(((mine ^ bit) & ~(bit - 1)) * columns, HDIM)
            away_ref[0] = out_ref[:, pl.ds(at, bit * columns)]


def backward_kernel(
    last_bits,
    q_ref,
    k_ref,
    v_ref,
    before_ref,
    kept_k_ref,
    kept_v_ref,
    got_k_ref,
    got_v_ref,
    probs_ref,
    attn_ref,
    grad_ref,
    dq_ref,
    dk_ref,
    dv_ref,
    kept_ref,
    sent_ref,
    dprobs_ref,
    dscores_ref,
    rounded_ref,
):
    rows = q_ref.shape[0]
    blocks = rows // BLK
    heads = q_ref.shape[1] // HDIM
    for local in range(heads):
        cols = slice(local * HDIM, (local + 1) * HDIM)
        v_ext = jnp.concatenate([before_ref[BLK:, cols], v_ref[:, cols]], axis=0)
        v_sink = sink_of(kept_v_ref[:, cols], got_v_ref[:, cols], last_bits[1])
        dprobs_ref[local, :, 2 * BLK :] = dot(grad_ref[:, cols], v_sink, 1, 1)
        for number in range(blocks):
            here = slice(number * BLK, (number + 1) * BLK)
            there = slice(number * BLK, (number + WIN) * BLK)
            dprobs_ref[local, here, : 2 * BLK] = dot(grad_ref[here, cols], v_ext[there], 1, 1)
    for local in range(heads):
        cols = slice(local * HDIM, (local + 1) * HDIM)
        for row in range(0, rows, ROWS_STEP):
            at = slice(row, row + ROWS_STEP)
            delta = jnp.sum(
                grad_ref[at, cols].astype(F32) * attn_ref[at, cols].astype(F32),
                axis=1,
                keepdims=True,
            )
            probs = probs_ref[local, at]
            dscores_ref[local, at] = (probs * (dprobs_ref[local, at] - delta)).astype(BF16)
            rounded_ref[local, at] = probs.astype(BF16)
    odd = (lax.axis_index("ctx") & 1) != 0
    for local in range(heads):
        cols = slice(local * HDIM, (local + 1) * HDIM)
        q = q_ref[:, cols]
        grad = grad_ref[:, cols]
        k_ext = jnp.concatenate([before_ref[:BLK, cols], k_ref[:, cols]], axis=0)
        k_sink = sink_of(kept_k_ref[:, cols], got_k_ref[:, cols], last_bits[0])
        dq_sink = dot(dscores_ref[local, :, 2 * BLK :], k_sink, 1, 0)
        for number in range(blocks):
            here = slice(number * BLK, (number + 1) * BLK)
            there = slice(number * BLK, (number + WIN) * BLK)
            dq = dot(dscores_ref[local, here, : 2 * BLK], k_ext[there], 1, 0)
            dq_ref[here, cols] = ((dq + dq_sink[here]) * ROOT).astype(BF16)
        dsink_k = dot(dscores_ref[local, :, 2 * BLK :], q, 0, 0) * ROOT
        dsink_v = dot(rounded_ref[local, :, 2 * BLK :], grad, 0, 0)
        kept_ref[:, cols] = jnp.where(odd, dsink_v, dsink_k)
        sent_ref[:, cols] = jnp.where(odd, dsink_k, dsink_v).astype(BF16)
        for number in range(blocks):
            here = slice(number * BLK, (number + 1) * BLK)
            own = slice(BLK, 2 * BLK)
            dk = dot(dscores_ref[local, here, own], q[here], 0, 0)
            dv = dot(rounded_ref[local, here, own], grad[here], 0, 0)
            if number + 1 < blocks:
                above = slice((number + 1) * BLK, (number + 2) * BLK)
                dk += dot(dscores_ref[local, above, :BLK], q[above], 0, 0)
                dv += dot(rounded_ref[local, above, :BLK], grad[above], 0, 0)
            dk_ref[here, cols] = dk * ROOT
            dv_ref[here, cols] = dv


def next_kernel(
    blocks, k_ref, v_ref, next_ref, stats_ref, pattern_ref, dk_ref, dv_ref, out_k_ref, out_v_ref
):
    heads = k_ref.shape[1] // HDIM
    total_heads = pl.num_programs(0) * heads
    block = (lax.axis_index("ctx") + 1) * blocks
    inside = jnp.minimum(block, pattern_ref.shape[2] - 1)
    lane = lax.broadcasted_iota(jnp.int32, (BLK, BLK), 1)
    stats = stats_ref[...]

    def column(index):
        return jnp.sum(jnp.where(lane == index, stats, 0.0), axis=1, keepdims=True)

    for local in range(heads):
        cols = slice(local * HDIM, (local + 1) * HDIM)
        head = pl.program_id(0) * heads + local
        top, inverse, delta = (column(head + kind * total_heads) for kind in range(3))
        q, grad = next_ref[:BLK, cols], next_ref[BLK:, cols]
        scores = dot(q, k_ref[:, cols], 1, 1)
        reached = jnp.logical_and(pattern_ref[0, head, inside, 1] == 1, block >= 2)
        probs = jnp.exp2((scores - top) * (ROOT * LOG2_E)) * inverse
        probs = jnp.where(reached, probs, 0.0)
        dprobs = dot(grad, v_ref[:, cols], 1, 1)
        dscores = (probs * (dprobs - delta)).astype(BF16)
        dk = dk_ref[:, cols] + dot(dscores, q, 0, 0) * ROOT
        dv = dv_ref[:, cols] + dot(probs.astype(BF16), grad, 0, 0)
        out_k_ref[:, cols] = dk.astype(BF16)
        out_v_ref[:, cols] = dv.astype(BF16)


def ends_kernel(k_first_ref, v_first_ref, k_last_ref, v_last_ref, k_ref, v_ref, last_ref):
    k_ref[...] = k_first_ref[...]
    v_ref[...] = v_first_ref[...]
    last_ref[:BLK] = k_last_ref[...]
    last_ref[BLK:] = v_last_ref[...]


def ends_of(k, v):
    rows, width = k.shape
    first = pl.BlockSpec((BLK, width), lambda step: (0, 0))
    last = pl.BlockSpec((BLK, width), lambda step: (rows // BLK - 1, 0))
    shape = jax.ShapeDtypeStruct
    return pl.pallas_call(
        ends_kernel,
        grid=(1,),
        in_specs=[first, first, last, last],
        out_specs=[first, first, pl.BlockSpec((2 * BLK, width), lambda step: (0, 0))],
        out_shape=[
            shape((BLK, width), BF16),
            shape((BLK, width), BF16),
            shape((2 * BLK, width), BF16),
        ],
        name="ends",
    )(k, v, k, v)


def head_spec(rows):
    return pl.BlockSpec((rows, HEADS_STEP * HDIM), lambda step: (0, step))


def whole_smem(shape):
    return pl.BlockSpec(shape, lambda *_: (0,) * len(shape), memory_space=pltpu.SMEM)


def attention_specs(rows):
    return [
        head_spec(rows),
        head_spec(rows),
        head_spec(rows),
        head_spec(2 * BLK),
        head_spec(BLK),
        head_spec(BLK),
        head_spec(BLK),
        head_spec(BLK),
    ]


def probs_spec(rows):
    return pl.BlockSpec((HEADS_STEP, rows, (WIN + 1) * BLK), lambda step: (step, 0, 0))


def attention_forward(count, last_bits, q, k, v, before, sinks, pattern, grad):
    rows, width = q.shape
    heads = width // HDIM
    away = [bit * width // count for bit in reversed(bits_of(count))]
    shape = jax.ShapeDtypeStruct
    return pl.pallas_call(
        functools.partial(forward_kernel, count, last_bits),
        grid=(heads // HEADS_STEP,),
        in_specs=attention_specs(rows) + [whole_smem(pattern.shape), head_spec(rows)],
        out_specs=[
            pl.BlockSpec((rows, width), lambda step: (0, 0)),
            probs_spec(rows),
            pl.BlockSpec((BLK, BLK), lambda step: (0, 0)),
            *(pl.BlockSpec((1, rows, one), lambda step: (0, 0, 0)) for one in away),
        ],
        out_shape=[
            shape((rows, width), BF16),
            shape((heads, rows, (WIN + 1) * BLK), F32),
            shape((BLK, BLK), F32),
            *(shape((1, rows, one), BF16) for one in away),
        ],
        scratch_shapes=[
            pltpu.VMEM((HEADS_STEP, rows, (WIN + 1) * BLK), F32),
            pltpu.VMEM((HEADS_STEP, rows, (WIN + 1) * BLK), BF16),
        ],
        name="attention_forward",
    )(q, k, v, before, *sinks, pattern, grad)


def attention_backward(last_bits, q, k, v, before, sinks, probs, attn, grad):
    rows, width = q.shape
    shape = jax.ShapeDtypeStruct
    scratch = (HEADS_STEP, rows, (WIN + 1) * BLK)
    return pl.pallas_call(
        functools.partial(backward_kernel, last_bits),
        grid=(width // (HEADS_STEP * HDIM),),
        in_specs=attention_specs(rows) + [probs_spec(rows), head_spec(rows), head_spec(rows)],
        out_specs=[
            head_spec(rows),
            head_spec(rows),
            head_spec(rows),
            head_spec(BLK),
            head_spec(BLK),
        ],
        out_shape=[
            shape((rows, width), BF16),
            shape((rows, width), F32),
            shape((rows, width), F32),
            shape((BLK, width), F32),
            shape((BLK, width), BF16),
        ],
        scratch_shapes=[
            pltpu.VMEM(scratch, F32),
            pltpu.VMEM(scratch, BF16),
            pltpu.VMEM(scratch, BF16),
        ],
        name="attention_backward",
    )(q, k, v, before, *sinks, probs, attn, grad)


def next_backward(k, v, following, stats, pattern, dk, dv):
    rows, width = k.shape
    blocks = rows // BLK
    shape = jax.ShapeDtypeStruct((rows, width), BF16)
    last = pl.BlockSpec((BLK, HEADS_STEP * HDIM), lambda step: (blocks - 1, step))
    return pl.pallas_call(
        functools.partial(next_kernel, blocks),
        grid=(width // (HEADS_STEP * HDIM),),
        in_specs=[
            last,
            last,
            head_spec(2 * BLK),
            pl.BlockSpec((BLK, BLK), lambda step: (0, 0)),
            whole_smem(pattern.shape),
            last,
            last,
        ],
        out_specs=[last, last],
        out_shape=[shape, shape],
        name="next_backward",
    )(k, v, following, stats, pattern, dk, dv)


def grad_attn_kernel(count, *refs):
    cot_ref, q_ref, pieces, out_ref, back_ref = refs[0], refs[1], refs[2:-2], refs[-2], refs[-1]
    mine = lax.axis_index("dp")
    number = 0
    for piece in pieces:
        depth = piece.shape[1]
        for slot in range(piece.shape[0]):
            at = pl.multiple_of((mine ^ order_of(count)[number]) * depth, HDIM)
            out_ref[:, pl.ds(at, depth)] = dot(cot_ref[...], piece[slot], 1, 1).astype(BF16)
            number += 1
    back_ref[:BLK] = q_ref[:BLK]
    back_ref[BLK:] = out_ref[:BLK]


def projected_kernel(count, *refs):
    attn_ref, pieces, out_ref = refs[0], refs[1:-1], refs[-1]
    mine = lax.axis_index("dp")
    total, number = None, 0
    for piece in pieces:
        depth = piece.shape[1]
        for slot in range(piece.shape[0]):
            at = pl.multiple_of((mine ^ order_of(count)[number]) * depth, HDIM)
            term = dot(attn_ref[:, pl.ds(at, depth)], piece[slot], 1, 0)
            total = term if total is None else total + term
            number += 1
    out_ref[...] = total.astype(BF16)


def weight_grad_kernel(scale, pairs, *refs):
    lefts, rights = refs[:pairs], refs[pairs : 2 * pairs]
    keep_ref, away_ref, left_scr = refs[2 * pairs :]
    mine = lax.axis_index("dp")
    features = left_scr.shape[0]
    rows = lefts[0].shape[-2]

    @pl.when(pl.program_id(0) == 0)
    def _():
        number = 0
        for left in lefts:
            shared = left.shape[-1] // features
            at = pl.multiple_of((mine & (shared - 1)) * features, HDIM)
            for slot in range(left.shape[0]):
                left_scr[:, number * rows : (number + 1) * rows] = left[
                    slot, :, pl.ds(at, features)
                ].T
                number += 1

    columns = keep_ref.shape[2]
    upper = (lax.axis_index("ctx") & 1) != 0
    for out_ref, here in ((away_ref, jnp.where(upper, 0, columns)), (keep_ref, jnp.where(upper, columns, 0))):
        here = pl.multiple_of(here, HDIM)
        right = jnp.concatenate(
            [one[slot, :, pl.ds(here, columns)] for one in rights for slot in range(one.shape[0])],
            axis=0,
        )
        out_ref[0] = (dot(left_scr[...], right, 1, 0) * scale).astype(out_ref.dtype)


def plain_weight_grad_kernel(scale, pairs, *refs):
    lefts, rights, out_ref = refs[:pairs], refs[pairs : 2 * pairs], refs[-1]
    mine = lax.axis_index("dp")
    features = out_ref.shape[1]
    total = None
    for left, right in zip(lefts, rights):
        at = pl.multiple_of((mine & (left.shape[-1] // features - 1)) * features, HDIM)
        for slot in range(left.shape[0]):
            term = dot(left[slot, :, pl.ds(at, features)], right[slot], 0, 0)
            total = term if total is None else total + term
    out_ref[0] = total * scale


def grad_attn_of(cot, q, pieces, count):
    rows = cot.shape[0]
    width = count * pieces[0].shape[1]
    return pl.pallas_call(
        functools.partial(grad_attn_kernel, count),
        out_shape=[
            jax.ShapeDtypeStruct((rows, width), BF16),
            jax.ShapeDtypeStruct((2 * BLK, width), BF16),
        ],
        name="grad_attn",
    )(cot, q, *pieces)


def projected_of(attn, pieces, count):
    return pl.pallas_call(
        functools.partial(projected_kernel, count),
        out_shape=jax.ShapeDtypeStruct((attn.shape[0], pieces[0].shape[2]), BF16),
        name="projected",
    )(attn, *pieces)


def weight_grad_of(attn_pieces, cot_pieces, scale, document_count, count):
    features = attn_pieces[0].shape[2] // document_count
    wanted = cot_pieces[0].shape[2] // count
    if wanted % HDIM:
        return plain_weight_grad_of(attn_pieces, cot_pieces, scale, document_count, count)
    rows = attn_pieces[0].shape[1]
    places = len(bits_of(count)) - 1

    def reversed_bits(step):
        return sum(((step >> place) & 1) << (places - 1 - place) for place in range(places))

    out = pl.BlockSpec((1, features, wanted), lambda step: (reversed_bits(step), 0, 0))
    return pl.pallas_call(
        functools.partial(weight_grad_kernel, scale, len(attn_pieces)),
        grid=(count // 2,),
        in_specs=[pl.BlockSpec(memory_space=pltpu.VMEM) for _ in attn_pieces]
        + [pl.BlockSpec(c.shape[:2] + (2 * wanted,), lambda step: (0, 0, step)) for c in cot_pieces],
        out_specs=[out, out],
        out_shape=[
            jax.ShapeDtypeStruct((count // 2, features, wanted), F32),
            jax.ShapeDtypeStruct((count // 2, features, wanted), BF16),
        ],
        scratch_shapes=[pltpu.VMEM((features, document_count * rows), BF16)],
        name="weight_grad",
    )(*attn_pieces, *cot_pieces)


def plain_weight_grad_of(attn_pieces, cot_pieces, scale, document_count, count):
    features = attn_pieces[0].shape[2] // document_count
    wanted = cot_pieces[0].shape[2] // count
    columns = HDIM
    chunks = cot_pieces[0].shape[2] // columns
    terms = pl.pallas_call(
        functools.partial(plain_weight_grad_kernel, scale, len(attn_pieces)),
        grid=(chunks,),
        in_specs=[pl.BlockSpec(a.shape, lambda step: (0, 0, 0)) for a in attn_pieces]
        + [pl.BlockSpec(c.shape[:2] + (columns,), lambda step: (0, 0, step)) for c in cot_pieces],
        out_specs=pl.BlockSpec((1, features, columns), lambda step: (step, 0, 0)),
        out_shape=jax.ShapeDtypeStruct((chunks, features, columns), F32),
        name="weight_grad",
    )(*attn_pieces, *cot_pieces)
    terms = terms.reshape(chunks, features, columns // wanted, wanted)
    places = len(bits_of(count))
    terms = jnp.swapaxes(terms, 1, 2).reshape((2,) * places + (features, wanted))
    terms = terms.transpose(tuple(reversed(range(places))) + (places, places + 1))
    terms = terms.reshape(2, count // 2, features, wanted)
    here = lax.axis_index("ctx") & 1
    keep = lax.dynamic_index_in_dim(terms, here, 0, keepdims=False)
    return keep, lax.dynamic_index_in_dim(terms, 1 - here, 0, keepdims=False).astype(BF16)


def finish_kernel(part_k_ref, part_v_ref, own_k_ref, own_v_ref, total_ref, got_ref, out_k_ref, out_v_ref):
    del part_k_ref, part_v_ref
    first = jnp.logical_and(lax.axis_index("ctx") == 0, pl.program_id(0) == 0)
    out_k_ref[...] = (own_k_ref[...] + jnp.where(first, total_ref[...], 0.0)).astype(BF16)
    out_v_ref[...] = (own_v_ref[...] + jnp.where(first, got_ref[...].astype(F32), 0.0)).astype(BF16)


def finish(part_k, part_v, own_k, own_v, total, got):
    rows, width = own_k.shape
    block = pl.BlockSpec((BLK, width), lambda step: (step, 0))
    same = pl.BlockSpec((BLK, width), lambda step: (0, 0))
    whole = pl.BlockSpec(memory_space=pl.ANY)
    shape = jax.ShapeDtypeStruct(part_k.shape, BF16)
    return pl.pallas_call(
        finish_kernel,
        grid=(rows // BLK - 1,),
        in_specs=[whole, whole, block, block, same, pl.BlockSpec(memory_space=pltpu.VMEM)],
        out_specs=[block, block],
        out_shape=[shape, shape],
        input_output_aliases={0: 0, 1: 1},
        name="finish",
    )(part_k, part_v, own_k, own_v, total, got)


def bits_of(count):
    return [1 << place for place in range(count.bit_length() - 1)]


def order_of(count):
    order = [0]
    for bit in reversed(bits_of(count)):
        order += [one ^ bit for one in order]
    return order


def swap(value, axis, count, bit):
    return lax.ppermute(value, axis, [(one, one ^ bit) for one in range(count)])


def gather_pieces(value, axis, count, away=None):
    pieces = [value[None]]
    for place, bit in enumerate(reversed(bits_of(count))):
        got = []
        for number, one in enumerate(pieces):
            got.append(swap(away[place] if away and not number else one, axis, count, bit))
        pieces += got
    return pieces


def spread_first(value, axis, count, order):
    mine = lax.axis_index(axis)
    covered = 0
    got = None
    for place, bit in enumerate(order):
        if place:
            value = jnp.where((mine & order[place - 1]) != 0, got, value)
        pairs = [(one, one | bit) for one in range(count) if one & ~covered == 0]
        got = lax.ppermute(value, axis, pairs)
        covered |= bit
    return value, got


def sum_to_first(kept, sent, axis, count):
    bits = bits_of(count)
    kept = kept + swap(sent, axis, count, 1).astype(F32)
    done = 0
    for bit in bits[1:]:
        pairs = [(one, one ^ bit) for one in range(count) if one & bit and one & done == 0]
        kept = kept + lax.ppermute(kept.astype(BF16), axis, pairs).astype(F32)
        done |= bit
    return kept, lax.ppermute(kept.astype(BF16), axis, [(1, 0)])


def sum_scatter(keep, away, axis, count):
    mine = lax.axis_index(axis)
    bits = bits_of(count)
    keep = keep.reshape((2,) * (len(bits) - 1) + keep.shape[1:])
    away = away.reshape(keep.shape)
    for place, bit in enumerate(bits):
        if place:
            here = jnp.where((mine & bit) != 0, 1, 0)
            away = lax.dynamic_index_in_dim(keep, 1 - here, 0, keepdims=False).astype(BF16)
            keep = lax.dynamic_index_in_dim(keep, here, 0, keepdims=False)
        keep = keep + swap(away, axis, count, bit).astype(F32)
    return keep


def body(context_count, document_count, queries, keys, values, cotangent, proj_weight, pattern):
    q, k, v, cot = queries[0], keys[0], values[0], cotangent[0]
    rows, _ = q.shape
    bits = bits_of(context_count)
    far_first = bits[:0:-1]

    first_k, first_v, last = ends_of(k, v)
    before = lax.ppermute(last, "ctx", [(one, one + 1) for one in range(context_count - 1)])
    order_k, order_v = bits[:1] + far_first, far_first + bits[:1]
    last_bits = order_k[-1], order_v[-1]
    kept_k, got_k = spread_first(first_k, "ctx", context_count, order_k)
    kept_v, got_v = spread_first(first_v, "ctx", context_count, order_v)
    sinks = kept_k, kept_v, got_k, got_v
    weights = gather_pieces(proj_weight, "dp", document_count)
    cots = gather_pieces(cot, "dp", document_count)
    back = [(one + 1, one) for one in range(context_count - 1)]
    grad_attn, following = grad_attn_of(cot, q, weights, document_count)
    following = lax.ppermute(following, "ctx", back)
    attn, probs, stats, *away = attention_forward(document_count, last_bits, q, k, v, before, sinks, pattern, grad_attn)
    attns = gather_pieces(attn, "dp", document_count, away)
    stats = lax.ppermute(stats, "ctx", back)
    dq, dk, dv, kept, sent = attention_backward(
        last_bits, q, k, v, before, sinks, probs, attn, grad_attn
    )
    total, got = sum_to_first(kept, sent, "ctx", context_count)
    projected = projected_of(attn, weights, document_count)
    scale = float(rows * context_count * document_count) ** (-0.5)
    keep, send = weight_grad_of(attns, cots, scale, document_count, context_count)
    grad_proj = sum_scatter(keep, send, "ctx", context_count)
    grad_k, grad_v = next_backward(k, v, following, stats, pattern, dk, dv)
    grad_k, grad_v = finish(grad_k, grad_v, dk, dv, total, got)
    return projected[None], dq[None], grad_k[None], grad_v[None], grad_proj


def solution(mesh):
    sizes = mesh.shape["ctx"], mesh.shape["dp"]
    return jax.shard_map(
        functools.partial(body, *sizes),
        mesh=mesh,
        in_specs=(
            P("dp", "ctx", None),
            P("dp", "ctx", None),
            P("dp", "ctx", None),
            P("dp", "ctx", None),
            P("dp", None),
            P("dp", None, None, None),
        ),
        out_specs=(
            P("dp", "ctx", None),
            P("dp", "ctx", None),
            P("dp", "ctx", None),
            P("dp", "ctx", None),
            P("dp", "ctx"),
        ),
        check_vma=False,
    )
```

```python
import functools
import math

import jax
import jax.numpy as jnp
from jax import lax
from jax.experimental import pallas as pl
from jax.experimental.pallas import tpu as pltpu
from jax.sharding import PartitionSpec as P


HDIM = 128
BLK = 128

WIN = 2
HEADS_STEP = 4
NEAR_K, NEAR_V = 0, 2

ROWS_STEP = 64
LOG2_E = math.log2(math.e)
MASKED = -1e30
ROOT = HDIM ** (-0.5)
F32 = jnp.float32
BF16 = jnp.bfloat16


def dot(left, right, left_dim, right_dim):
    return lax.dot_general(
        left, right, (((left_dim,), (right_dim,)), ((), ())), preferred_element_type=F32
    )


def sink_of(kept, got, bit):
    return jnp.where((lax.axis_index("ctx") & bit) != 0, got, kept)


def softmax_rows(scores_ref, at, pattern_ref, head, block, first_row):
    scores = scores_ref[at]
    shape = (scores.shape[0], BLK)
    causal = lax.broadcasted_iota(jnp.int32, shape, 1) <= (
        lax.broadcasted_iota(jnp.int32, shape, 0) + first_row
    )
    reached = jnp.logical_and(pattern_ref[0, head, block, 1] == 1, block >= 2)
    before = jnp.where(reached, scores[:, :BLK], MASKED)
    own = jnp.where(jnp.logical_and(causal, block >= 1), scores[:, BLK : 2 * BLK], MASKED)
    first = jnp.where(jnp.logical_or(causal, block >= 1), scores[:, 2 * BLK :], MASKED)
    top = jnp.max(jnp.maximum(jnp.maximum(before, own), first), axis=1, keepdims=True)
    parts = [jnp.exp2((one - top) * (ROOT * LOG2_E)) for one in (before, own, first)]
    total = jnp.sum(parts[0] + parts[1] + parts[2], axis=1, keepdims=True)
    return parts, top, 1.0 / total


def forward_kernel(
    count,
    last_bits,
    q_ref,
    k_ref,
    v_ref,
    before_ref,
    kept_k_ref,
    kept_v_ref,
    got_k_ref,
    got_v_ref,
    pattern_ref,
    grad_ref,
    out_ref,
    probs_ref,
    stats_ref,
    *rest,
):
    away_refs, (scores_ref, rounded_ref) = rest[:-2], rest[-2:]
    rows = q_ref.shape[0]
    blocks = rows // BLK
    heads = q_ref.shape[1] // HDIM
    total_heads = out_ref.shape[1] // HDIM
    first_block = lax.axis_index("ctx") * blocks
    first_head = pl.program_id(0) * heads

    @pl.when(pl.program_id(0) == 0)
    def _():
        stats_ref[...] = jnp.zeros_like(stats_ref)

    for local in range(heads):
        cols = slice(local * HDIM, (local + 1) * HDIM)
        k_ext = jnp.concatenate([before_ref[:BLK, cols], k_ref[:, cols]], axis=0)
        k_sink = sink_of(kept_k_ref[:, cols], got_k_ref[:, cols], last_bits[0])
        scores_ref[local, :, 2 * BLK :] = dot(q_ref[:, cols], k_sink, 1, 1)
        for number in range(blocks):
            here = slice(number * BLK, (number + 1) * BLK)
            there = slice(number * BLK, (number + WIN) * BLK)
            scores_ref[local, here, : 2 * BLK] = dot(q_ref[here, cols], k_ext[there], 1, 1)
    lane = lax.broadcasted_iota(jnp.int32, (ROWS_STEP, BLK), 1)
    for local in range(heads):
        cols = slice(local * HDIM, (local + 1) * HDIM)
        head = first_head + local
        for row in range(0, rows, ROWS_STEP):
            at = slice(row, row + ROWS_STEP)
            parts, top, inverse = softmax_rows(
                scores_ref.at[local], at, pattern_ref, head, first_block + row // BLK, row % BLK
            )
            for place, part in enumerate(parts):
                there = slice(place * BLK, (place + 1) * BLK)
                part = part * inverse
                probs_ref[local, at, there] = part
                rounded_ref[local, at, there] = part.astype(BF16)
            if row < BLK:
                stats = stats_ref[at]
                stats = jnp.where(lane == head, top, stats)
                stats_ref[at] = jnp.where(lane == head + total_heads, inverse, stats)
    for local in range(heads):
        cols = slice(local * HDIM, (local + 1) * HDIM)
        head = first_head + local
        v_ext = jnp.concatenate([before_ref[BLK:, cols], v_ref[:, cols]], axis=0)
        v_sink = sink_of(kept_v_ref[:, cols], got_v_ref[:, cols], last_bits[1])
        from_sink = dot(rounded_ref[local, :, 2 * BLK :], v_sink, 1, 0)
        for number in range(blocks):
            here = slice(number * BLK, (number + 1) * BLK)
            there = slice(number * BLK, (number + WIN) * BLK)
            near = dot(rounded_ref[local, here, : 2 * BLK], v_ext[there], 1, 0)
            attended = (near + from_sink[here]).astype(BF16)
            out_ref[here, pl.ds(pl.multiple_of(head * HDIM, HDIM), HDIM)] = attended
            if number == 0:
                delta = jnp.sum(
                    grad_ref[:BLK, cols].astype(F32) * attended.astype(F32), axis=1, keepdims=True
                )
                wide = lax.broadcasted_iota(jnp.int32, (BLK, BLK), 1)
                stats_ref[...] = jnp.where(wide == head + 2 * total_heads, delta, stats_ref[...])

    @pl.when(pl.program_id(0) == pl.num_programs(0) - 1)
    def _():
        mine = lax.axis_index("dp")
        columns = out_ref.shape[1] // count
        for bit, away_ref in zip(reversed(bits_of(count)), away_refs):
            at = pl.multiple_of(((mine ^ bit) & ~(bit - 1)) * columns, HDIM)
            away_ref[0] = out_ref[:, pl.ds(at, bit * columns)]


def backward_kernel(
    last_bits,
    q_ref,
    k_ref,
    v_ref,
    before_ref,
    kept_k_ref,
    kept_v_ref,
    got_k_ref,
    got_v_ref,
    probs_ref,
    attn_ref,
    grad_ref,
    dq_ref,
    dk_ref,
    dv_ref,
    kept_ref,
    sent_ref,
    dprobs_ref,
    dscores_ref,
    rounded_ref,
):
    rows = q_ref.shape[0]
    blocks = rows // BLK
    heads = q_ref.shape[1] // HDIM
    for local in range(heads):
        cols = slice(local * HDIM, (local + 1) * HDIM)
        v_ext = jnp.concatenate([before_ref[BLK:, cols], v_ref[:, cols]], axis=0)
        v_sink = sink_of(kept_v_ref[:, cols], got_v_ref[:, cols], last_bits[1])
        dprobs_ref[local, :, 2 * BLK :] = dot(grad_ref[:, cols], v_sink, 1, 1)
        for number in range(blocks):
            here = slice(number * BLK, (number + 1) * BLK)
            there = slice(number * BLK, (number + WIN) * BLK)
            dprobs_ref[local, here, : 2 * BLK] = dot(grad_ref[here, cols], v_ext[there], 1, 1)
    for local in range(heads):
        cols = slice(local * HDIM, (local + 1) * HDIM)
        for row in range(0, rows, ROWS_STEP):
            at = slice(row, row + ROWS_STEP)
            delta = jnp.sum(
                grad_ref[at, cols].astype(F32) * attn_ref[at, cols].astype(F32),
                axis=1,
                keepdims=True,
            )
            probs = probs_ref[local, at]
            dscores_ref[local, at] = (probs * (dprobs_ref[local, at] - delta)).astype(BF16)
            rounded_ref[local, at] = probs.astype(BF16)
    odd = (lax.axis_index("ctx") & 1) != 0
    for local in range(heads):
        cols = slice(local * HDIM, (local + 1) * HDIM)
        q = q_ref[:, cols]
        grad = grad_ref[:, cols]
        k_ext = jnp.concatenate([before_ref[:BLK, cols], k_ref[:, cols]], axis=0)
        k_sink = sink_of(kept_k_ref[:, cols], got_k_ref[:, cols], last_bits[0])
        dq_sink = dot(dscores_ref[local, :, 2 * BLK :], k_sink, 1, 0)
        for number in range(blocks):
            here = slice(number * BLK, (number + 1) * BLK)
            there = slice(number * BLK, (number + WIN) * BLK)
            dq = dot(dscores_ref[local, here, : 2 * BLK], k_ext[there], 1, 0)
            dq_ref[here, cols] = ((dq + dq_sink[here]) * ROOT).astype(BF16)
        dsink_k = dot(dscores_ref[local, :, 2 * BLK :], q, 0, 0) * ROOT
        dsink_v = dot(rounded_ref[local, :, 2 * BLK :], grad, 0, 0)
        kept_ref[:, cols] = jnp.where(odd, dsink_v, dsink_k)
        sent_ref[:, cols] = jnp.where(odd, dsink_k, dsink_v).astype(BF16)
        for number in range(blocks):
            here = slice(number * BLK, (number + 1) * BLK)
            own = slice(BLK, 2 * BLK)
            dk = dot(dscores_ref[local, here, own], q[here], 0, 0)
            dv = dot(rounded_ref[local, here, own], grad[here], 0, 0)
            if number + 1 < blocks:
                above = slice((number + 1) * BLK, (number + 2) * BLK)
                dk += dot(dscores_ref[local, above, :BLK], q[above], 0, 0)
                dv += dot(rounded_ref[local, above, :BLK], grad[above], 0, 0)
            dk_ref[here, cols] = dk * ROOT
            dv_ref[here, cols] = dv


def next_kernel(
    blocks, k_ref, v_ref, next_ref, stats_ref, pattern_ref, dk_ref, dv_ref, out_k_ref, out_v_ref
):
    heads = k_ref.shape[1] // HDIM
    total_heads = pl.num_programs(0) * heads
    block = (lax.axis_index("ctx") + 1) * blocks
    inside = jnp.minimum(block, pattern_ref.shape[2] - 1)
    lane = lax.broadcasted_iota(jnp.int32, (BLK, BLK), 1)
    stats = stats_ref[...]

    def column(index):
        return jnp.sum(jnp.where(lane == index, stats, 0.0), axis=1, keepdims=True)

    for local in range(heads):
        cols = slice(local * HDIM, (local + 1) * HDIM)
        head = pl.program_id(0) * heads + local
        top, inverse, delta = (column(head + kind * total_heads) for kind in range(3))
        q, grad = next_ref[:BLK, cols], next_ref[BLK:, cols]
        scores = dot(q, k_ref[:, cols], 1, 1)
        reached = jnp.logical_and(pattern_ref[0, head, inside, 1] == 1, block >= 2)
        probs = jnp.exp2((scores - top) * (ROOT * LOG2_E)) * inverse
        probs = jnp.where(reached, probs, 0.0)
        dprobs = dot(grad, v_ref[:, cols], 1, 1)
        dscores = (probs * (dprobs - delta)).astype(BF16)
        dk = dk_ref[:, cols] + dot(dscores, q, 0, 0) * ROOT
        dv = dv_ref[:, cols] + dot(probs.astype(BF16), grad, 0, 0)
        out_k_ref[:, cols] = dk.astype(BF16)
        out_v_ref[:, cols] = dv.astype(BF16)


def ends_kernel(k_first_ref, v_first_ref, k_last_ref, v_last_ref, k_ref, v_ref, last_ref):
    k_ref[...] = k_first_ref[...]
    v_ref[...] = v_first_ref[...]
    last_ref[:BLK] = k_last_ref[...]
    last_ref[BLK:] = v_last_ref[...]


def ends_of(k, v):
    rows, width = k.shape
    first = pl.BlockSpec((BLK, width), lambda step: (0, 0))
    last = pl.BlockSpec((BLK, width), lambda step: (rows // BLK - 1, 0))
    shape = jax.ShapeDtypeStruct
    return pl.pallas_call(
        ends_kernel,
        grid=(1,),
        in_specs=[first, first, last, last],
        out_specs=[first, first, pl.BlockSpec((2 * BLK, width), lambda step: (0, 0))],
        out_shape=[
            shape((BLK, width), BF16),
            shape((BLK, width), BF16),
            shape((2 * BLK, width), BF16),
        ],
        name="ends",
    )(k, v, k, v)


def head_spec(rows):
    return pl.BlockSpec((rows, HEADS_STEP * HDIM), lambda step: (0, step))


def whole_smem(shape):
    return pl.BlockSpec(shape, lambda *_: (0,) * len(shape), memory_space=pltpu.SMEM)


def attention_specs(rows):
    return [
        head_spec(rows),
        head_spec(rows),
        head_spec(rows),
        head_spec(2 * BLK),
        head_spec(BLK),
        head_spec(BLK),
        head_spec(BLK),
        head_spec(BLK),
    ]


def probs_spec(rows):
    return pl.BlockSpec((HEADS_STEP, rows, (WIN + 1) * BLK), lambda step: (step, 0, 0))


def attention_forward(count, last_bits, q, k, v, before, sinks, pattern, grad):
    rows, width = q.shape
    heads = width // HDIM
    away = [bit * width // count for bit in reversed(bits_of(count))]
    shape = jax.ShapeDtypeStruct
    return pl.pallas_call(
        functools.partial(forward_kernel, count, last_bits),
        grid=(heads // HEADS_STEP,),
        in_specs=attention_specs(rows) + [whole_smem(pattern.shape), head_spec(rows)],
        out_specs=[
            pl.BlockSpec((rows, width), lambda step: (0, 0)),
            probs_spec(rows),
            pl.BlockSpec((BLK, BLK), lambda step: (0, 0)),
            *(pl.BlockSpec((1, rows, one), lambda step: (0, 0, 0)) for one in away),
        ],
        out_shape=[
            shape((rows, width), BF16),
            shape((heads, rows, (WIN + 1) * BLK), F32),
            shape((BLK, BLK), F32),
            *(shape((1, rows, one), BF16) for one in away),
        ],
        scratch_shapes=[
            pltpu.VMEM((HEADS_STEP, rows, (WIN + 1) * BLK), F32),
            pltpu.VMEM((HEADS_STEP, rows, (WIN + 1) * BLK), BF16),
        ],
        name="attention_forward",
    )(q, k, v, before, *sinks, pattern, grad)


def attention_backward(last_bits, q, k, v, before, sinks, probs, attn, grad):
    rows, width = q.shape
    shape = jax.ShapeDtypeStruct
    scratch = (HEADS_STEP, rows, (WIN + 1) * BLK)
    return pl.pallas_call(
        functools.partial(backward_kernel, last_bits),
        grid=(width // (HEADS_STEP * HDIM),),
        in_specs=attention_specs(rows) + [probs_spec(rows), head_spec(rows), head_spec(rows)],
        out_specs=[
            head_spec(rows),
            head_spec(rows),
            head_spec(rows),
            head_spec(BLK),
            head_spec(BLK),
        ],
        out_shape=[
            shape((rows, width), BF16),
            shape((rows, width), F32),
            shape((rows, width), F32),
            shape((BLK, width), F32),
            shape((BLK, width), BF16),
        ],
        scratch_shapes=[
            pltpu.VMEM(scratch, F32),
            pltpu.VMEM(scratch, BF16),
            pltpu.VMEM(scratch, BF16),
        ],
        name="attention_backward",
    )(q, k, v, before, *sinks, probs, attn, grad)


def next_backward(k, v, following, stats, pattern, dk, dv):
    rows, width = k.shape
    blocks = rows // BLK
    shape = jax.ShapeDtypeStruct((rows, width), BF16)
    last = pl.BlockSpec((BLK, HEADS_STEP * HDIM), lambda step: (blocks - 1, step))
    return pl.pallas_call(
        functools.partial(next_kernel, blocks),
        grid=(width // (HEADS_STEP * HDIM),),
        in_specs=[
            last,
            last,
            head_spec(2 * BLK),
            pl.BlockSpec((BLK, BLK), lambda step: (0, 0)),
            whole_smem(pattern.shape),
            last,
            last,
        ],
        out_specs=[last, last],
        out_shape=[shape, shape],
        name="next_backward",
    )(k, v, following, stats, pattern, dk, dv)


def grad_attn_kernel(count, *refs):
    cot_ref, q_ref, pieces, out_ref, back_ref = refs[0], refs[1], refs[2:-2], refs[-2], refs[-1]
    mine = lax.axis_index("dp")
    number = 0
    for piece in pieces:
        depth = piece.shape[1]
        for slot in range(piece.shape[0]):
            at = pl.multiple_of((mine ^ order_of(count)[number]) * depth, HDIM)
            out_ref[:, pl.ds(at, depth)] = dot(cot_ref[...], piece[slot], 1, 1).astype(BF16)
            number += 1
    back_ref[:BLK] = q_ref[:BLK]
    back_ref[BLK:] = out_ref[:BLK]


def projected_kernel(count, *refs):
    attn_ref, pieces, out_ref = refs[0], refs[1:-1], refs[-1]
    mine = lax.axis_index("dp")
    total, number = None, 0
    for piece in pieces:
        depth = piece.shape[1]
        for slot in range(piece.shape[0]):
            at = pl.multiple_of((mine ^ order_of(count)[number]) * depth, HDIM)
            term = dot(attn_ref[:, pl.ds(at, depth)], piece[slot], 1, 0)
            total = term if total is None else total + term
            number += 1
    out_ref[...] = total.astype(BF16)


def weight_grad_kernel(scale, pairs, *refs):
    lefts, rights = refs[:pairs], refs[pairs : 2 * pairs]
    keep_ref, away_ref, left_scr = refs[2 * pairs :]
    mine = lax.axis_index("dp")
    features = left_scr.shape[0]
    rows = lefts[0].shape[-2]

    @pl.when(pl.program_id(0) == 0)
    def _():
        number = 0
        for left in lefts:
            shared = left.shape[-1] // features
            at = pl.multiple_of((mine & (shared - 1)) * features, HDIM)
            for slot in range(left.shape[0]):
                left_scr[:, number * rows : (number + 1) * rows] = left[
                    slot, :, pl.ds(at, features)
                ].T
                number += 1

    columns = keep_ref.shape[2]
    upper = (lax.axis_index("ctx") & 1) != 0
    for out_ref, here in ((away_ref, jnp.where(upper, 0, columns)), (keep_ref, jnp.where(upper, columns, 0))):
        here = pl.multiple_of(here, HDIM)
        right = jnp.concatenate(
            [one[slot, :, pl.ds(here, columns)] for one in rights for slot in range(one.shape[0])],
            axis=0,
        )
        out_ref[0] = (dot(left_scr[...], right, 1, 0) * scale).astype(out_ref.dtype)


def plain_weight_grad_kernel(scale, pairs, *refs):
    lefts, rights, out_ref = refs[:pairs], refs[pairs : 2 * pairs], refs[-1]
    mine = lax.axis_index("dp")
    features = out_ref.shape[1]
    total = None
    for left, right in zip(lefts, rights):
        at = pl.multiple_of((mine & (left.shape[-1] // features - 1)) * features, HDIM)
        for slot in range(left.shape[0]):
            term = dot(left[slot, :, pl.ds(at, features)], right[slot], 0, 0)
            total = term if total is None else total + term
    out_ref[0] = total * scale


def grad_attn_of(cot, q, pieces, count):
    rows = cot.shape[0]
    width = count * pieces[0].shape[1]
    return pl.pallas_call(
        functools.partial(grad_attn_kernel, count),
        out_shape=[
            jax.ShapeDtypeStruct((rows, width), BF16),
            jax.ShapeDtypeStruct((2 * BLK, width), BF16),
        ],
        name="grad_attn",
    )(cot, q, *pieces)


def projected_of(attn, pieces, count):
    return pl.pallas_call(
        functools.partial(projected_kernel, count),
        out_shape=jax.ShapeDtypeStruct((attn.shape[0], pieces[0].shape[2]), BF16),
        name="projected",
    )(attn, *pieces)


def weight_grad_of(attn_pieces, cot_pieces, scale, document_count, count):
    features = attn_pieces[0].shape[2] // document_count
    wanted = cot_pieces[0].shape[2] // count
    if wanted % HDIM:
        return plain_weight_grad_of(attn_pieces, cot_pieces, scale, document_count, count)
    rows = attn_pieces[0].shape[1]
    places = len(bits_of(count)) - 1

    def reversed_bits(step):
        return sum(((step >> place) & 1) << (places - 1 - place) for place in range(places))

    out = pl.BlockSpec((1, features, wanted), lambda step: (reversed_bits(step), 0, 0))
    return pl.pallas_call(
        functools.partial(weight_grad_kernel, scale, len(attn_pieces)),
        grid=(count // 2,),
        in_specs=[pl.BlockSpec(memory_space=pltpu.VMEM) for _ in attn_pieces]
        + [pl.BlockSpec(c.shape[:2] + (2 * wanted,), lambda step: (0, 0, step)) for c in cot_pieces],
        out_specs=[out, out],
        out_shape=[
            jax.ShapeDtypeStruct((count // 2, features, wanted), F32),
            jax.ShapeDtypeStruct((count // 2, features, wanted), BF16),
        ],
        scratch_shapes=[pltpu.VMEM((features, document_count * rows), BF16)],
        name="weight_grad",
    )(*attn_pieces, *cot_pieces)


def plain_weight_grad_of(attn_pieces, cot_pieces, scale, document_count, count):
    features = attn_pieces[0].shape[2] // document_count
    wanted = cot_pieces[0].shape[2] // count
    columns = HDIM
    chunks = cot_pieces[0].shape[2] // columns
    terms = pl.pallas_call(
        functools.partial(plain_weight_grad_kernel, scale, len(attn_pieces)),
        grid=(chunks,),
        in_specs=[pl.BlockSpec(a.shape, lambda step: (0, 0, 0)) for a in attn_pieces]
        + [pl.BlockSpec(c.shape[:2] + (columns,), lambda step: (0, 0, step)) for c in cot_pieces],
        out_specs=pl.BlockSpec((1, features, columns), lambda step: (step, 0, 0)),
        out_shape=jax.ShapeDtypeStruct((chunks, features, columns), F32),
        name="weight_grad",
    )(*attn_pieces, *cot_pieces)
    terms = terms.reshape(chunks, features, columns // wanted, wanted)
    places = len(bits_of(count))
    terms = jnp.swapaxes(terms, 1, 2).reshape((2,) * places + (features, wanted))
    terms = terms.transpose(tuple(reversed(range(places))) + (places, places + 1))
    terms = terms.reshape(2, count // 2, features, wanted)
    here = lax.axis_index("ctx") & 1
    keep = lax.dynamic_index_in_dim(terms, here, 0, keepdims=False)
    return keep, lax.dynamic_index_in_dim(terms, 1 - here, 0, keepdims=False).astype(BF16)


def finish_kernel(part_k_ref, part_v_ref, own_k_ref, own_v_ref, total_ref, got_ref, out_k_ref, out_v_ref):
    del part_k_ref, part_v_ref
    first = jnp.logical_and(lax.axis_index("ctx") == 0, pl.program_id(0) == 0)
    out_k_ref[...] = (own_k_ref[...] + jnp.where(first, total_ref[...], 0.0)).astype(BF16)
    out_v_ref[...] = (own_v_ref[...] + jnp.where(first, got_ref[...].astype(F32), 0.0)).astype(BF16)


def finish(part_k, part_v, own_k, own_v, total, got):
    rows, width = own_k.shape
    block = pl.BlockSpec((BLK, width), lambda step: (step, 0))
    same = pl.BlockSpec((BLK, width), lambda step: (0, 0))
    whole = pl.BlockSpec(memory_space=pl.ANY)
    shape = jax.ShapeDtypeStruct(part_k.shape, BF16)
    return pl.pallas_call(
        finish_kernel,
        grid=(rows // BLK - 1,),
        in_specs=[whole, whole, block, block, same, pl.BlockSpec(memory_space=pltpu.VMEM)],
        out_specs=[block, block],
        out_shape=[shape, shape],
        input_output_aliases={0: 0, 1: 1},
        name="finish",
    )(part_k, part_v, own_k, own_v, total, got)


def bits_of(count):
    return [1 << place for place in range(count.bit_length() - 1)]


def order_of(count):
    order = [0]
    for bit in reversed(bits_of(count)):
        order += [one ^ bit for one in order]
    return order


def swap(value, axis, count, bit):
    return lax.ppermute(value, axis, [(one, one ^ bit) for one in range(count)])


def gather_pieces(value, axis, count, away=None):
    pieces = [value[None]]
    for place, bit in enumerate(reversed(bits_of(count))):
        got = []
        for number, one in enumerate(pieces):
            got.append(swap(away[place] if away and not number else one, axis, count, bit))
        pieces += got
    return pieces


def spread_orders(count):
    near, far_first = bits_of(count)[:1], bits_of(count)[:0:-1]
    return tuple(far_first[:at] + near + far_first[at:] for at in (NEAR_K, NEAR_V))


def spread_first(value, axis, count, order):
    mine = lax.axis_index(axis)
    covered = 0
    got = None
    for place, bit in enumerate(order):
        if place:
            value = jnp.where((mine & order[place - 1]) != 0, got, value)
        pairs = [(one, one | bit) for one in range(count) if one & ~covered == 0]
        got = lax.ppermute(value, axis, pairs)
        covered |= bit
    return value, got


def sum_to_first(kept, sent, axis, count):
    bits = bits_of(count)
    kept = kept + swap(sent, axis, count, 1).astype(F32)
    done = 0
    for bit in bits[1:]:
        pairs = [(one, one ^ bit) for one in range(count) if one & bit and one & done == 0]
        kept = kept + lax.ppermute(kept.astype(BF16), axis, pairs).astype(F32)
        done |= bit
    return kept, lax.ppermute(kept.astype(BF16), axis, [(1, 0)])


def sum_scatter(keep, away, axis, count):
    mine = lax.axis_index(axis)
    bits = bits_of(count)
    keep = keep.reshape((2,) * (len(bits) - 1) + keep.shape[1:])
    away = away.reshape(keep.shape)
    for place, bit in enumerate(bits):
        if place:
            here = jnp.where((mine & bit) != 0, 1, 0)
            away = lax.dynamic_index_in_dim(keep, 1 - here, 0, keepdims=False).astype(BF16)
            keep = lax.dynamic_index_in_dim(keep, here, 0, keepdims=False)
        keep = keep + swap(away, axis, count, bit).astype(F32)
    return keep


def body(context_count, document_count, queries, keys, values, cotangent, proj_weight, pattern):
    q, k, v, cot = queries[0], keys[0], values[0], cotangent[0]
    rows, _ = q.shape

    first_k, first_v, last = ends_of(k, v)
    before = lax.ppermute(last, "ctx", [(one, one + 1) for one in range(context_count - 1)])
    order_k, order_v = spread_orders(context_count)
    last_bits = order_k[-1], order_v[-1]
    kept_k, got_k = spread_first(first_k, "ctx", context_count, order_k)
    kept_v, got_v = spread_first(first_v, "ctx", context_count, order_v)
    sinks = kept_k, kept_v, got_k, got_v
    weights = gather_pieces(proj_weight, "dp", document_count)
    cots = gather_pieces(cot, "dp", document_count)
    back = [(one + 1, one) for one in range(context_count - 1)]
    grad_attn, following = grad_attn_of(cot, q, weights, document_count)
    following = lax.ppermute(following, "ctx", back)
    attn, probs, stats, *away = attention_forward(document_count, last_bits, q, k, v, before, sinks, pattern, grad_attn)
    attns = gather_pieces(attn, "dp", document_count, away)
    stats = lax.ppermute(stats, "ctx", back)
    dq, dk, dv, kept, sent = attention_backward(
        last_bits, q, k, v, before, sinks, probs, attn, grad_attn
    )
    total, got = sum_to_first(kept, sent, "ctx", context_count)
    projected = projected_of(attn, weights, document_count)
    scale = float(rows * context_count * document_count) ** (-0.5)
    keep, send = weight_grad_of(attns, cots, scale, document_count, context_count)
    grad_proj = sum_scatter(keep, send, "ctx", context_count)
    grad_k, grad_v = next_backward(k, v, following, stats, pattern, dk, dv)
    grad_k, grad_v = finish(grad_k, grad_v, dk, dv, total, got)
    return projected[None], dq[None], grad_k[None], grad_v[None], grad_proj


def solution(mesh):
    sizes = mesh.shape["ctx"], mesh.shape["dp"]
    return jax.shard_map(
        functools.partial(body, *sizes),
        mesh=mesh,
        in_specs=(
            P("dp", "ctx", None),
            P("dp", "ctx", None),
            P("dp", "ctx", None),
            P("dp", "ctx", None),
            P("dp", None),
            P("dp", None, None, None),
        ),
        out_specs=(
            P("dp", "ctx", None),
            P("dp", "ctx", None),
            P("dp", "ctx", None),
            P("dp", "ctx", None),
            P("dp", "ctx"),
        ),
        check_vma=False,
    )
```
